128 devices in a mesh: gx: 8 (over x, core), gy: 16 (over y, z).
Axes of the slice: x: 4, y: 4, z: 4, core: 2. Of those that a mesh axis runs over, the one named last changes fastest.
Arguments:
- blocks: float32 [16384, 4, 4096], P(('gx', 'gy')), may hold values from -0.75 to 0.75
- prolong: float32 [16384, 4096], P(('gx', 'gy')), may hold values from -2 to 2
- columns: int32 [16384, 4], P(('gx', 'gy')), may hold values from 0 to 16383, as said below
- aggregate: int32 [16384], P(('gx', 'gy')), may hold values from 0 to 8191, as said below
- column_slot: int32 [16384, 4], P(('gx', 'gy')), may hold values from 0 to 6, as said below
- owner_row: int32 [8192], P(('gx', 'gy')), may hold values from 0 to 8191, as said below
Outputs:
- merged_panel: float32 [16384, 7, 4096], P(('gx', 'gy'))
The draws below stay inside these ranges and needn't reach their ends.
Inputs may be any that keep to these rules, and one draw needn't show every extreme that they name: `columns`: row i lists i first, then 3 distinct other blocks within 3 of i. `aggregate`: fine rows 4p+2 to 4p+5 (mod 16384) form coarse rows 2p and 2p+1 in that order, the first taking 1 to 3 of them. column_slot[i, k] = (aggregate[columns[i, k]] - aggregate[i] + 3) mod 8192. `owner_row`: a permutation. Coarse row I is held by device I // 64 and stored on device owner_row[I] // 64, a device with the same gy index; every device stores exactly 64 rows, and at most 9 of the rows held by one device go to one device, a bound reached in every draw.
All inputs are finite; a program needn't handle non-finite values.
Results may differ from the reference program's by a relative error of at most 0.0003.
Values sent between devices are 32-bit elements; how exact they have to be, the bound alone decides.
A program may use at most 192 MiB of HBM per device.

```python
import jax
import jax.numpy as jnp
from jax import lax

BS = 64
NNZ = 4
REACH = 3
SLOTS = 7
NB_DEV = 128
NCD = 64
FINE = 16384
COARSE = 8192
N_GX = 8
N_GY = 16


def aggregate_of(key):
    split_at = jax.random.randint(jax.random.fold_in(key, 11), (COARSE // 2,), 1, 4).astype(jnp.int32)
    block_index = jnp.arange(FINE, dtype=jnp.int32)
    shifted = jnp.remainder(block_index - 2, FINE)
    pair_index = shifted // 4
    position = shifted % 4
    return (2 * pair_index + (position >= split_at[pair_index]).astype(jnp.int32)).astype(jnp.int32)


def columns_of(key):
    block_index = jnp.arange(FINE, dtype=jnp.int32)
    offsets = jnp.concatenate([jnp.arange(-REACH, 0, dtype=jnp.int32), jnp.arange(1, REACH + 1, dtype=jnp.int32)])
    targets = block_index[:, None] + offsets[None, :]
    inside = (targets >= 0) & (targets < FINE)
    scores = jax.random.randint(jax.random.fold_in(key, 12), (FINE, 2 * REACH), 0, 4096).astype(jnp.int32)
    scores = scores * 8 + jnp.arange(2 * REACH, dtype=jnp.int32)[None, :]
    scores = jnp.where(inside, scores, -1)
    chosen = lax.top_k(scores, NNZ - 1)[1]
    picked = jnp.take_along_axis(targets, chosen, axis=1)
    return jnp.concatenate([block_index[:, None], picked], axis=1).astype(jnp.int32)


def draw_columns(key, part):
    return columns_of(key)


def draw_aggregate(key, part):
    return aggregate_of(key)


def draw_column_slot(key, part):
    groups = aggregate_of(key)
    linked = columns_of(key)
    return jnp.remainder(groups[linked] - groups[:, None] + REACH, COARSE).astype(jnp.int32)


def draw_owner_row(key, part):
    size_gx = N_GX
    size_gy = N_GY
    share = NCD // size_gx
    order_gx = jax.random.permutation(jax.random.fold_in(key, 13), size_gx)
    bumps = jnp.zeros((size_gx,), jnp.int32).at[order_gx[0]].add(1).at[order_gx[1]].add(-1)
    source = jnp.arange(size_gx, dtype=jnp.int32)
    counts = share + bumps[jnp.remainder(source[None, :] - source[:, None], size_gx)]
    running = jnp.cumsum(counts, axis=1)
    row_index = jnp.arange(NCD, dtype=jnp.int32)
    labels = jnp.sum((running[:, None, :] <= row_index[None, :, None]).astype(jnp.int32), axis=2)
    spread = jnp.broadcast_to(labels[:, None, :], (size_gx, size_gy, NCD))
    shuffled = jax.random.permutation(jax.random.fold_in(key, 14), spread, axis=2, independent=True)
    onehot = (shuffled[..., None] == source[None, None, None, :]).astype(jnp.int32)
    rank_in = jnp.sum((jnp.cumsum(onehot, axis=2) - onehot) * onehot, axis=3)
    earlier = jnp.cumsum(counts, axis=0) - counts
    source_grid = jnp.broadcast_to(source[:, None, None], (size_gx, size_gy, NCD))
    slot_index = earlier[source_grid, shuffled] + rank_in
    column_gy = jnp.arange(size_gy, dtype=jnp.int32)[None, :, None]
    stored = (shuffled * size_gy + column_gy) * NCD + slot_index
    return stored.reshape(-1).astype(jnp.int32)


def level_of(own_key, extent, pieces, least, largest):
    loudness, own = 1.0, jax.random.fold_in(own_key, 6)
    for dim, shards_of in pieces:
        heights = jnp.exp(jax.random.uniform(jax.random.fold_in(own, dim), (shards_of,), jnp.float32, least / len(pieces), largest / len(pieces)))
        loudness = loudness * jnp.repeat(heights, extent[dim] // shards_of).reshape([-1 if axis == dim else 1 for axis in range(len(extent))])
    return loudness


def normal_values(stream_key, dims, scale, limit, cuts=(), kind=jnp.bfloat16):
    loudness = level_of(stream_key, dims, cuts, -0.22, 0.18) if cuts else 1.0
    entries = jax.random.normal(stream_key, dims, jnp.float32) * scale * loudness
    return jnp.minimum(jnp.maximum(entries, -limit), limit).astype(kind)


def setup_inputs(seed: int = 0) -> dict:
    key_of = jax.random.split(jax.random.key(seed), 7)
    blocks = normal_values(key_of[0], (FINE, NNZ, BS * BS), BS ** -0.5, 0.75, ((0, 128),), jnp.float32)
    prolong = normal_values(key_of[1], (FINE, BS * BS), 0.35, 2.0, ((0, 128),), jnp.float32)
    columns = draw_columns(jax.random.fold_in(key_of[6], 71), 0)
    aggregate = draw_aggregate(jax.random.fold_in(key_of[6], 71), 0)
    column_slot = draw_column_slot(jax.random.fold_in(key_of[6], 71), 0)
    owner_row = draw_owner_row(jax.random.fold_in(key_of[6], 71), 0)
    return dict(blocks=blocks, prolong=prolong, columns=columns, aggregate=aggregate, column_slot=column_slot, owner_row=owner_row)


def galerkin_terms(block_rows, left_blocks, right_blocks):
    count = block_rows.shape[0]
    matrix = block_rows.reshape(count, NNZ, BS, BS)
    left_q = left_blocks.reshape(count, BS, BS)
    right_q = right_blocks.reshape(count, NNZ, BS, BS)
    product = jnp.einsum("ikab,ikbc->ikac", matrix, right_q, precision=lax.Precision.HIGHEST)
    sandwich = jnp.einsum("iba,ikbc->ikac", left_q, product, precision=lax.Precision.HIGHEST)
    return sandwich.reshape(count * NNZ, BS * BS)


def reference(blocks, prolong, columns, aggregate, column_slot, owner_row):
    slab_count = FINE // NB_DEV

    def add_slab(accumulated, slab_index):
        slab_start = (slab_index * NB_DEV).astype(jnp.int32)
        slab_blocks = lax.dynamic_slice_in_dim(blocks, slab_start, NB_DEV, 0)
        slab_columns = lax.dynamic_slice_in_dim(columns, slab_start, NB_DEV, 0)
        left_blocks = lax.dynamic_slice_in_dim(prolong, slab_start, NB_DEV, 0)
        slab_aggregate = lax.dynamic_slice_in_dim(aggregate, slab_start, NB_DEV, 0)
        slab_slots = lax.dynamic_slice_in_dim(column_slot, slab_start, NB_DEV, 0)
        right_blocks = prolong[slab_columns]
        values = galerkin_terms(slab_blocks, left_blocks, right_blocks)
        target = (slab_aggregate[:, None] * SLOTS + slab_slots).reshape(-1).astype(jnp.int32)
        return accumulated.at[target].add(values), None

    start_sum = jnp.zeros((COARSE * SLOTS, BS * BS), jnp.float32)
    accumulated, _ = lax.scan(add_slab, start_sum, jnp.arange(slab_count, dtype=jnp.int32))
    coarse = accumulated.reshape(COARSE, SLOTS, BS * BS)
    placed = jnp.zeros_like(coarse).at[owner_row].set(coarse)
    pair_count = COARSE // (2 * NCD)
    paired = placed.reshape(pair_count, 1, 2 * NCD, SLOTS, BS * BS)
    merged = jnp.broadcast_to(paired, (pair_count, 2, 2 * NCD, SLOTS, BS * BS))
    return merged.reshape(2 * COARSE, SLOTS, BS * BS)
```

```python
import functools

import jax
import jax.numpy as jnp
from jax import lax
from jax.experimental import pallas as pl
from jax.experimental.pallas import tpu as pltpu
from jax.sharding import PartitionSpec as P

BS = 64
NNZ = 4
SLOTS = 7
MESH = pl.DeviceIdType.MESH
ANY = pl.BlockSpec(memory_space=pl.ANY)
SMEM = pl.BlockSpec(memory_space=pltpu.SMEM)
VMEM = pl.BlockSpec(memory_space=pltpu.VMEM)

ROW_CAP = 9
ROW_BLOCKS = 6
CAP = ROW_CAP * ROW_BLOCKS
META = 128
NB = 128
NC = 64
EXT = NB + 6
F32 = jnp.float32
BF16 = jnp.bfloat16


def split(x):
    hi = x.astype(BF16)
    return hi, (x - hi.astype(F32)).astype(BF16)


def halo_kernel(n_gx, n_gy, blocks, prolong, ints, nblocks, nright, nleft, nints, send, recv):
    me = lax.axis_index("gx") * n_gy + lax.axis_index("gy")
    total = n_gx * n_gy
    up = lax.rem(me + 1, total)
    down = lax.rem(me + total - 1, total)
    up = (up // n_gy, lax.rem(up, n_gy))
    down = (down // n_gy, lax.rem(down, n_gy))
    barrier = pltpu.get_barrier_semaphore()
    for other in (up, down):
        pl.semaphore_signal(barrier, inc=1, device_id=other, device_id_type=MESH)
    pl.semaphore_wait(barrier, 2)
    copies = []
    plan = (
        (ints, nints, down),
        (prolong.at[15], nleft, up),
        (prolong.at[0], nright, down),
        (blocks.at[pl.ds(0, 2)], nblocks, down),
    )
    for n, (src, dst, to) in enumerate(plan):
        copy = pltpu.make_async_remote_copy(
            src_ref=src,
            dst_ref=dst,
            send_sem=send.at[n],
            recv_sem=recv.at[n],
            device_id=to,
            device_id_type=MESH,
        )
        copy.start()
        copies.append(copy)
    for copy in copies:
        copy.wait()


def halo(n_gx, n_gy, blocks, prolong, ints):
    return pl.pallas_call(
        functools.partial(halo_kernel, n_gx, n_gy),
        out_shape=(
            jax.ShapeDtypeStruct((2, 128, 128), F32),
            jax.ShapeDtypeStruct((256, 128), F32),
            jax.ShapeDtypeStruct((256, 128), F32),
            jax.ShapeDtypeStruct((8, 128), jnp.int32),
        ),
        in_specs=[ANY] * 3,
        out_specs=[ANY] * 4,
        scratch_shapes=[pltpu.SemaphoreType.DMA((4,)), pltpu.SemaphoreType.DMA((4,))],
        compiler_params=pltpu.CompilerParams(collective_id=0, has_side_effects=True),
        name="halo",
    )(blocks, prolong, ints)


def coarse_kernel(
    code_ref, col_ref, dest_ref, local_ref, blocks, nblocks, prolong, nright, nleft,
    bucket, meta, natural, weights, rows, acc, cnt,
):
    n_dest = cnt.shape[0]

    @pl.loop(0, n_dest)
    def _(d):
        cnt[d] = 0

        @pl.loop(0, META, unroll=8)
        def _(b):
            meta[d, 0, b] = -1

    def prepare(x, flat):
        natural[pl.ds(0, 32, 2), :] = flat[:, :BS]
        natural[pl.ds(1, 32, 2), :] = flat[:, BS:]
        hi, lo = split(natural[...])
        weights[x] = jnp.concatenate([hi, hi, lo], axis=0)
        hi, lo = split(jnp.concatenate([flat[:, :BS], flat[:, BS:]], axis=0))
        rows[x] = jnp.concatenate([hi, lo, hi], axis=0)

    prepare(0, nleft[pl.ds(7, 32, 8), :])
    for r in range(5):
        prepare(NB + 1 + r, nright[pl.ds(r, 32, 8), :])

    @pl.loop(0, NB // 8)
    def _(g):
        for r in range(8):
            prepare(g * 8 + r + 1, prolong[g, pl.ds(r, 32, 8), :])

    def fine_row(e, ablock, acc_base):
        parts = [ablock(k) for k in range(NNZ)]
        top = jnp.concatenate([part[:, :BS] for part in parts], axis=1)
        bottom = jnp.concatenate([part[:, BS:] for part in parts], axis=1)
        hi, lo = split(jnp.concatenate([top, bottom], axis=0))
        right = jnp.concatenate([hi, hi, lo], axis=0)
        left = lax.dot_general(
            rows[e + 3], right, (((0,), (0,)), ((), ())), preferred_element_type=F32
        )
        for k in range(NNZ):
            hi, lo = split(left[:, k * BS : (k + 1) * BS])
            value = jnp.dot(
                jnp.concatenate([hi, lo, hi], axis=1),
                weights[col_ref[e * NNZ + k]],
                preferred_element_type=F32,
            )
            code = code_ref[e * NNZ + k]
            acc[code] = acc[code] + value

    def pair(p, ablocks):
        acc[...] = jnp.zeros_like(acc)
        for t in range(4):
            fine_row(p * 4 + t, ablocks[t], 0)
        mask = 0
        for t in range(16):
            mask = mask | (1 << code_ref[p * 16 + t])
        for c in range(2 * SLOTS):
            used = (mask >> c) & 1
            dest = dest_ref[p * 2 + c // SLOTS]
            local = local_ref[p * 2 + c // SLOTS]
            position = cnt[dest]

            @pl.when(used == 1)
            def _():
                cnt[dest] = position + 1
                meta[dest, 0, position] = local * 8 + c % SLOTS
                even = acc[c, pl.ds(0, 32, 2), :]
                odd = acc[c, pl.ds(1, 32, 2), :]
                bucket[dest, position] = jnp.concatenate([even, odd], axis=1)

    def own(e):
        return lambda k: blocks[e + 2, pl.ds(k, 32, 4), :]

    def near(n):
        return lambda k: nblocks[n, pl.ds(k, 32, 4), :]

    @pl.loop(0, NC // 2 - 1)
    def _(p):
        pair(p, [own(p * 4 + t) for t in range(4)])

    last = NC // 2 - 1
    pair(last, [own(last * 4), own(last * 4 + 1), near(0), near(1)])


def coarse_buckets(n_gx, code, col, dest, local, blocks, nblocks, prolong, nright, nleft):
    return pl.pallas_call(
        coarse_kernel,
        out_shape=(
            jax.ShapeDtypeStruct((n_gx, CAP, 32, 128), F32),
            jax.ShapeDtypeStruct((n_gx, 1, META), jnp.int32),
        ),
        in_specs=[SMEM] * 4 + [VMEM] * 5,
        out_specs=(VMEM, SMEM),
        scratch_shapes=[
            pltpu.VMEM((BS, BS), F32),
            pltpu.VMEM((EXT, 3 * BS, BS), BF16),
            pltpu.VMEM((EXT, 3 * BS, BS), BF16),
            pltpu.VMEM((2 * SLOTS, BS, BS), F32),
            pltpu.SMEM((n_gx,), jnp.int32),
        ],
        compiler_params=pltpu.CompilerParams(vmem_limit_bytes=56 << 20),
        name="coarse",
    )(code, col, dest, local, blocks, nblocks, prolong, nright, nleft)


ORDER = (1, 2, 6, 3, 7, 4, 5)


def route_kernel(bucket, meta, got, got_meta, pair, pair_meta, xs, xr, xms, xmr, zs, zr, zms, zmr):
    gx, gy = lax.axis_index("gx"), lax.axis_index("gy")
    n_gx = bucket.shape[0]
    other = lax.rem(gy, 2)
    partner = (gx, gy + 1 - 2 * other)
    peer = [None] * n_gx
    for k in range(1, n_gx):
        bits = 0
        for b in range(3):
            bit = lax.rem(gx // (1 << b), 2)
            bits = bits + ((1 - bit) if (k >> b) & 1 else bit) * (1 << b)
        peer[k] = bits
    barrier = pltpu.get_barrier_semaphore()
    for k in range(1, n_gx):
        pl.semaphore_signal(barrier, inc=1, device_id=(peer[k], gy), device_id_type=MESH)
    pl.semaphore_signal(barrier, inc=1, device_id=partner, device_id_type=MESH)
    pl.semaphore_wait(barrier, n_gx)

    def copy(src, dst, send, recv, to):
        return pltpu.make_async_remote_copy(
            src_ref=src, dst_ref=dst, send_sem=send, recv_sem=recv, device_id=to, device_id_type=MESH
        )

    def forward(k, src, src_meta):
        made = [
            copy(src_meta, pair_meta.at[k], zms.at[k], zmr.at[k], partner),
            copy(src, pair.at[k], zs.at[k], zr.at[k], partner),
        ]
        for c in made:
            c.start()
        return made

    onward = forward(0, bucket.at[gx], meta.at[gx])
    sent = {}
    for k in ORDER:
        to = (peer[k], gy)
        sent[k] = (
            copy(meta.at[peer[k]], got_meta.at[k - 1], xms.at[k - 1], xmr.at[k - 1], to),
            copy(bucket.at[peer[k]], got.at[k - 1], xs.at[k - 1], xr.at[k - 1], to),
        )
        for c in sent[k]:
            c.start()
    for k in ORDER:
        for c in sent[k]:
            c.wait_recv()
        onward += forward(k, got.at[k - 1], got_meta.at[k - 1])
    for k in ORDER:
        for c in sent[k]:
            c.wait_send()
    for c in onward:
        c.wait()


def route(n_gx, bucket, meta):
    data = lambda n: jax.ShapeDtypeStruct((n, CAP, 32, 128), F32)
    tags = lambda n: jax.ShapeDtypeStruct((n, 1, META), jnp.int32)
    sems = lambda n: pltpu.SemaphoreType.DMA((n,))
    return pl.pallas_call(
        route_kernel,
        out_shape=(data(n_gx - 1), tags(n_gx - 1), data(n_gx), tags(n_gx)),
        in_specs=[ANY] * 2,
        out_specs=[ANY] * 4,
        scratch_shapes=[sems(n_gx - 1)] * 4 + [sems(n_gx)] * 4,
        compiler_params=pltpu.CompilerParams(collective_id=1, has_side_effects=True),
        name="route",
    )(bucket, meta)


def unpack_body(n_gx, mine_tags, got_tags, pair_tags, where, mine, got, pair, out):
    out[...] = jnp.zeros_like(out)

    def place(tag_at, block_at, base):
        @pl.loop(0, CAP)
        def _(b):
            tag = tag_at(b)

            @pl.when(tag >= 0)
            def _():
                row = base + tag // 8
                out[lax.rem(tag, 8), row // 8, pl.ds(lax.rem(row, 8), 32, 8), :] = block_at(b)

    gx = where[0]
    place(lambda b: mine_tags[gx, 0, b], lambda b: mine[0, b], where[1])

    @pl.loop(0, n_gx - 1)
    def _(k):
        place(lambda b: got_tags[k, 0, b], lambda b: got[k, b], where[1])

    @pl.loop(0, n_gx)
    def _(k):
        place(lambda b: pair_tags[k, 0, b], lambda b: pair[k, b], where[2])


def unpack(n_gx, tags, got_tags, pair_tags, where, bucket, got, pair):
    grid_spec = pltpu.PrefetchScalarGridSpec(
        num_scalar_prefetch=4,
        grid=(1,),
        in_specs=[
            pl.BlockSpec((1, CAP, 32, 128), lambda i, a, b, c, w: (w[0], 0, 0, 0), pipeline_mode=pl.Buffered(1)),
            VMEM,
            VMEM,
        ],
        out_specs=VMEM,
    )
    return pl.pallas_call(
        functools.partial(unpack_body, n_gx),
        out_shape=jax.ShapeDtypeStruct((SLOTS, 16, 256, 128), F32),
        grid_spec=grid_spec,
        compiler_params=pltpu.CompilerParams(vmem_limit_bytes=60 << 20),
        name="unpack",
    )(tags, got_tags, pair_tags, where, bucket, got, pair)


def body(blocks, prolong, columns, aggregate, column_slot, owner_row):
    n_gx, n_gy = lax.axis_size("gx"), lax.axis_size("gy")
    gx, gy = lax.axis_index("gx"), lax.axis_index("gy")
    first = (gx * n_gy + gy) * NB
    fine = NB * n_gx * n_gy
    flat = blocks.reshape(NB, NNZ, 32, 128).transpose(0, 2, 1, 3).reshape(NB, 128, 128)
    q = prolong.reshape(16, 8, 32, 128).transpose(0, 2, 1, 3).reshape(16, 256, 128)
    code = (aggregate & 1)[:, None] * SLOTS + column_slot
    ints = jnp.concatenate([code[:2].reshape(-1), columns[:2].reshape(-1)])
    ints = jnp.broadcast_to(jnp.pad(ints, (0, 112))[None], (8, 128))
    nblocks, nright, nleft, nints = halo(n_gx, n_gy, flat, q, ints)
    code = jnp.concatenate([code[2:].reshape(-1), nints[0, :8]])
    col = jnp.concatenate([columns[2:].reshape(-1), nints[0, 8:16]])
    col = jnp.remainder(col - first + 1, fine)
    dest = owner_row // (NC * n_gy)
    local = owner_row % NC
    bucket, meta = coarse_buckets(n_gx, code, col, dest, local, flat, nblocks, q, nright, nleft)
    got, got_meta, pair, pair_meta = route(n_gx, bucket, meta)
    odd = gy % 2
    where = jnp.stack([gx, odd * NC, (1 - odd) * NC]).astype(jnp.int32)
    out = unpack(n_gx, meta, got_meta, pair_meta, where, bucket, got, pair)
    out = out.reshape(SLOTS, 16, 32, 8, 128).transpose(1, 3, 0, 2, 4)
    return out.reshape(NB, SLOTS, BS * BS)


def solution(mesh):
    placed = (
        P(("gx", "gy"), None, None),
        P(("gx", "gy"), None),
        P(("gx", "gy"), None),
        P(("gx", "gy")),
        P(("gx", "gy"), None),
        P(("gx", "gy")),
    )
    return jax.shard_map(
        body, mesh=mesh, in_specs=placed, out_specs=P(("gx", "gy"), None, None), check_vma=False
    )
```

```python
import functools

import jax
import jax.numpy as jnp
from jax import lax
from jax.experimental import pallas as pl
from jax.experimental.pallas import tpu as pltpu
from jax.sharding import PartitionSpec as P

BS = 64
NNZ = 4
SLOTS = 7
MESH = pl.DeviceIdType.MESH
ANY = pl.BlockSpec(memory_space=pl.ANY)
SMEM = pl.BlockSpec(memory_space=pltpu.SMEM)
VMEM = pl.BlockSpec(memory_space=pltpu.VMEM)

ROW_CAP = 9
ROW_BLOCKS = 6
CAP = ROW_CAP * ROW_BLOCKS
META = 128
NB = 128
NC = 64
EXT = NB + 6
F32 = jnp.float32
BF16 = jnp.bfloat16


def split(x):
    hi = x.astype(BF16)
    return hi, (x - hi.astype(F32)).astype(BF16)


def halo_kernel(n_gx, n_gy, *refs):
    n = len(refs) // 2
    sources, (send, recv) = refs[: n - 1], refs[-2:]
    targets = refs[n - 1 : -2]
    me = lax.axis_index("gx") * n_gy + lax.axis_index("gy")
    total = n_gx * n_gy
    up = lax.rem(me + 1, total)
    down = lax.rem(me + total - 1, total)
    up = (up // n_gy, lax.rem(up, n_gy))
    down = (down // n_gy, lax.rem(down, n_gy))
    blocks, prolong, columns, slots, aggregate = sources
    nblocks, nright, nleft, ncolumns, nslots, naggregate = targets
    barrier = pltpu.get_barrier_semaphore()
    for other in (up, down):
        pl.semaphore_signal(barrier, inc=1, device_id=other, device_id_type=MESH)
    pl.semaphore_wait(barrier, 2)
    copies = []
    plan = (
        (columns, ncolumns, down),
        (slots, nslots, down),
        (aggregate, naggregate, down),
        (prolong.at[15], nleft, up),
        (prolong.at[0], nright, down),
        (blocks.at[pl.ds(0, 2)], nblocks, down),
    )
    for n, (src, dst, to) in enumerate(plan):
        copy = pltpu.make_async_remote_copy(
            src_ref=src,
            dst_ref=dst,
            send_sem=send.at[n],
            recv_sem=recv.at[n],
            device_id=to,
            device_id_type=MESH,
        )
        copy.start()
        copies.append(copy)
    for copy in copies:
        copy.wait()


def halo(n_gx, n_gy, blocks, prolong, columns, slots, aggregate):
    return pl.pallas_call(
        functools.partial(halo_kernel, n_gx, n_gy),
        out_shape=(
            jax.ShapeDtypeStruct((2, 128, 128), F32),
            jax.ShapeDtypeStruct((256, 128), F32),
            jax.ShapeDtypeStruct((256, 128), F32),
            jax.ShapeDtypeStruct((NNZ, 128), jnp.int32),
            jax.ShapeDtypeStruct((NNZ, 128), jnp.int32),
            jax.ShapeDtypeStruct((1, 128), jnp.int32),
        ),
        in_specs=[ANY] * 5,
        out_specs=[ANY] * 6,
        scratch_shapes=[pltpu.SemaphoreType.DMA((6,)), pltpu.SemaphoreType.DMA((6,))],
        compiler_params=pltpu.CompilerParams(collective_id=0, has_side_effects=True),
        name="halo",
    )(blocks, prolong, columns, slots, aggregate)


PIECES = 8
COUNT = META - 1


def coarse_kernel(
    n_gx, n_gy, owner, blocks_hbm, nblocks, prolong, nright, nleft, own_ints, near_ints, bucket, meta,
    blocks, column, slot, parity, natural, weights, rows, lefts, sums, cnt, sems, isems,
):
    first = (lax.axis_index("gx") * n_gy + lax.axis_index("gy")) * NB
    fine = n_gx * n_gy * NB
    per = NB // PIECES
    for n, (table, own, near) in enumerate(zip((column, slot, parity), own_ints, near_ints)):
        pltpu.make_async_copy(own, table.at[0], isems.at[n, 0]).start()
        pltpu.make_async_copy(near, table.at[1], isems.at[n, 1]).start()

    def piece(n):
        part = pl.ds(n * per, per)
        return pltpu.make_async_copy(blocks_hbm.at[part], blocks.at[part], sems.at[n])

    last = pltpu.make_async_copy(nblocks, blocks.at[pl.ds(NB, 2)], sems.at[PIECES])
    for n in range(PIECES):
        piece(n).start()
    last.start()

    for d in range(n_gx):
        cnt[d] = 0
    low = lax.broadcasted_iota(jnp.int32, (32, 128), 1) < BS

    def prepare(x, flat):
        turned = pltpu.roll(flat, BS, 1)
        zero = jnp.zeros_like(flat)
        natural[0, pl.ds(0, 32, 2), :] = jnp.where(low, flat, zero)
        natural[0, pl.ds(1, 32, 2), :] = jnp.where(low, turned, zero)
        natural[1, pl.ds(0, 32, 2), :] = jnp.where(low, zero, turned)
        natural[1, pl.ds(1, 32, 2), :] = jnp.where(low, zero, flat)
        for side in range(2):
            hi, lo = split(natural[side])
            weights[x, side, 0] = hi
            weights[x, side, 1] = lo
        hi, lo = split(jnp.concatenate([flat[:, :BS], turned[:, :BS]], axis=0))
        rows[x] = jnp.concatenate([hi, lo, hi], axis=0)

    prepare(0, nleft[pl.ds(7, 32, 8), :])
    for r in range(5):
        prepare(NB + 1 + r, nright[pl.ds(r, 32, 8), :])

    @pl.loop(0, NB // 4)
    def _(g):
        for r in range(4):
            prepare(g * 4 + r + 1, prolong[g // 2, pl.ds(lax.rem(g, 2) * 4 + r, 32, 8), :])

    for n, (table, own, near) in enumerate(zip((column, slot, parity), own_ints, near_ints)):
        pltpu.make_async_copy(own, table.at[0], isems.at[n, 0]).wait()
        pltpu.make_async_copy(near, table.at[1], isems.at[n, 1]).wait()

    def at_row(table, i, k):
        return table[i // 128, k, lax.rem(i, 128)]

    def first_product(p):
        for t in range(4):
            i = p * 4 + t + 2
            parts = [blocks[i, pl.ds(k, 32, 4), :] for k in range(NNZ)]
            turned = [pltpu.roll(part, BS, 1) for part in parts]
            top = [jnp.where(low, parts[k], turned[k + 1]) for k in (0, 2)]
            bottom = [jnp.where(low, turned[k], parts[k + 1]) for k in (0, 2)]
            hi, lo = split(
                jnp.concatenate([jnp.concatenate(top, axis=1), jnp.concatenate(bottom, axis=1)], axis=0)
            )
            left = lax.dot_general(
                rows[i + 1],
                jnp.concatenate([hi, hi, lo], axis=0),
                (((0,), (0,)), ((), ())),
                preferred_element_type=F32,
            )
            hi, lo = split(left)
            for h in range(2):
                lanes = slice(h * 128, h * 128 + 128)
                lefts[t, h, :, :128] = hi[:, lanes]
                lefts[t, h, :, 128:] = lo[:, lanes]

    def second_product(p):
        values = []
        for t in range(4):
            i = p * 4 + t + 2
            for h in range(2):
                a, b = [
                    jnp.remainder(at_row(column, i, k) - first + 1, fine) for k in (2 * h, 2 * h + 1)
                ]
                both = jnp.concatenate(
                    [
                        jnp.concatenate([weights[a, 0, 0], weights[b, 1, 0]], axis=0),
                        jnp.concatenate([weights[a, 0, 1], weights[b, 1, 1]], axis=0),
                    ],
                    axis=1,
                )
                value = jnp.dot(
                    lefts[t, h], jnp.concatenate([both, both], axis=0), preferred_element_type=F32
                )
                values.append(value[:, :128] + value[:, 128:])
        return values

    def add_up(p, values):
        sums[...] = jnp.zeros_like(sums)
        mask = 0
        for t in range(4):
            i = p * 4 + t + 2
            second = lax.rem(at_row(parity, i, 0), 2) * SLOTS
            for k in range(NNZ):
                code = second + at_row(slot, i, k)
                mask = mask | (1 << code)
                lanes = slice(0, BS) if k % 2 == 0 else slice(BS, 128)
                sums[code, :, lanes] = sums[code, :, lanes] + values[t * 2 + k // 2][:, lanes]
        return mask

    def flush(p, mask):
        for r in range(2):
            row = owner[jnp.maximum(p * 2 + r, 0)]
            dest = row // (NC * n_gy)
            tag = lax.rem(row, NC) * 8
            start = cnt[dest]
            for s in range(SLOTS):
                c = r * SLOTS + s
                used = (mask >> c) & 1
                meta[dest, 0, start] = tag + s
                place = jnp.where(used == 1, start, CAP)
                start = start + used
                even = sums[c, pl.ds(0, 32, 2), :]
                odd = sums[c, pl.ds(1, 32, 2), :]
                bucket[dest, place] = jnp.where(low, even, pltpu.roll(odd, BS, 1)) + jnp.where(
                    low, pltpu.roll(even, BS, 1), odd
                )
            cnt[dest] = start

    piece(0).wait()
    first_product(0)

    def group(g, mask):
        @pl.when(g < PIECES - 1)
        def _():
            piece(g + 1).wait()

        @pl.when(g == PIECES - 1)
        def _():
            last.wait()

        def step(q, mask):
            p = g * 4 + q
            flush(p - 1, mask)
            values = second_product(p)
            mask = add_up(p, values)
            first_product(jnp.minimum(p + 1, NC // 2 - 1))
            return mask

        return lax.fori_loop(0, 4, step, mask)

    mask = lax.fori_loop(0, PIECES, group, jnp.int32(0))
    flush(NC // 2 - 1, mask)

    for d in range(n_gx):
        meta[d, 0, COUNT] = cnt[d]


def coarse_buckets(n_gx, n_gy, owner, blocks, nblocks, prolong, nright, nleft, own_ints, near_ints):
    def kernel(owner, blocks, nblocks, prolong, nright, nleft, c0, s0, a0, c1, s1, a1, *rest):
        coarse_kernel(
            n_gx, n_gy, owner, blocks, nblocks, prolong, nright, nleft, (c0, s0, a0), (c1, s1, a1), *rest
        )

    return pl.pallas_call(
        kernel,
        out_shape=(
            jax.ShapeDtypeStruct((n_gx, CAP + 2, 32, 128), F32),
            jax.ShapeDtypeStruct((n_gx, 1, META), jnp.int32),
        ),
        in_specs=[SMEM, ANY, ANY] + [VMEM] * 3 + [ANY] * 6,
        out_specs=(VMEM, SMEM),
        scratch_shapes=[
            pltpu.VMEM((NB + 2, 128, 128), F32),
            pltpu.SMEM((2, NNZ, 128), jnp.int32),
            pltpu.SMEM((2, NNZ, 128), jnp.int32),
            pltpu.SMEM((2, 1, 128), jnp.int32),
            pltpu.VMEM((2, BS, 128), F32),
            pltpu.VMEM((EXT, 2, 2, BS, 128), BF16),
            pltpu.VMEM((EXT, 3 * BS, BS), BF16),
            pltpu.VMEM((4, 2, BS, 256), BF16),
            pltpu.VMEM((2 * SLOTS, BS, 128), F32),
            pltpu.SMEM((n_gx,), jnp.int32),
            pltpu.SemaphoreType.DMA((PIECES + 1,)),
            pltpu.SemaphoreType.DMA((3, 2)),
        ],
        compiler_params=pltpu.CompilerParams(vmem_limit_bytes=56 << 20),
        name="coarse",
    )(owner, blocks, nblocks, prolong, nright, nleft, *own_ints, *near_ints)


ORDER = (1, 2, 6, 3, 7, 4, 5)


def route_kernel(bucket, meta, got, got_meta, pair, pair_meta, xs, xr, xms, xmr, zs, zr, zms, zmr):
    gx, gy = lax.axis_index("gx"), lax.axis_index("gy")
    n_gx = bucket.shape[0]
    other = lax.rem(gy, 2)
    partner = (gx, gy + 1 - 2 * other)
    peer = [None] * n_gx
    for k in range(1, n_gx):
        bits = 0
        for b in range(3):
            bit = lax.rem(gx // (1 << b), 2)
            bits = bits + ((1 - bit) if (k >> b) & 1 else bit) * (1 << b)
        peer[k] = bits
    barrier = pltpu.get_barrier_semaphore()
    for k in range(1, n_gx):
        pl.semaphore_signal(barrier, inc=1, device_id=(peer[k], gy), device_id_type=MESH)
    pl.semaphore_signal(barrier, inc=1, device_id=partner, device_id_type=MESH)
    pl.semaphore_wait(barrier, n_gx)

    def copy(src, dst, send, recv, to):
        return pltpu.make_async_remote_copy(
            src_ref=src, dst_ref=dst, send_sem=send, recv_sem=recv, device_id=to, device_id_type=MESH
        )

    def forward(k, src, src_meta):
        made = [
            copy(src_meta, pair_meta.at[k], zms.at[k], zmr.at[k], partner),
            copy(src, pair.at[k], zs.at[k], zr.at[k], partner),
        ]
        for c in made:
            c.start()
        return made

    onward = forward(0, bucket.at[gx, pl.ds(0, CAP)], meta.at[gx])
    sent = {}
    for k in ORDER:
        to = (peer[k], gy)
        sent[k] = (
            copy(meta.at[peer[k]], got_meta.at[k - 1], xms.at[k - 1], xmr.at[k - 1], to),
            copy(bucket.at[peer[k], pl.ds(0, CAP)], got.at[k - 1], xs.at[k - 1], xr.at[k - 1], to),
        )
        for c in sent[k]:
            c.start()
    for k in ORDER:
        for c in sent[k]:
            c.wait_recv()
        onward += forward(k, got.at[k - 1], got_meta.at[k - 1])
    for k in ORDER:
        for c in sent[k]:
            c.wait_send()
    for c in onward:
        c.wait()


def route(n_gx, bucket, meta):
    data = lambda n: jax.ShapeDtypeStruct((n, CAP, 32, 128), F32)
    tags = lambda n: jax.ShapeDtypeStruct((n, 1, META), jnp.int32)
    sems = lambda n: pltpu.SemaphoreType.DMA((n,))
    return pl.pallas_call(
        route_kernel,
        out_shape=(data(n_gx - 1), tags(n_gx - 1), data(n_gx), tags(n_gx)),
        in_specs=[ANY] * 2,
        out_specs=[ANY] * 4,
        scratch_shapes=[sems(n_gx - 1)] * 4 + [sems(n_gx)] * 4,
        compiler_params=pltpu.CompilerParams(collective_id=1, has_side_effects=True),
        name="route",
    )(bucket, meta)


STEP = 4


def unpack_kernel(n_gx, tags, got_tags, pair_tags, bucket, got, pair, out, stage, panel, sems, osems):
    gx, odd = lax.axis_index("gx"), lax.rem(lax.axis_index("gy"), 2)
    chunks = [(tags, gx, bucket.at[gx, pl.ds(0, CAP)])]
    chunks += [(got_tags, k, got.at[k]) for k in range(n_gx - 1)]
    chunks += [(pair_tags, k, pair.at[k]) for k in range(n_gx)]
    loads = [
        pltpu.make_async_copy(source, stage.at[c, pl.ds(0, CAP)], sems.at[c])
        for c, (_, _, source) in enumerate(chunks)
    ]
    for load in loads:
        load.start()

    @pl.loop(0, 16)
    def _(g):
        for s in range(SLOTS):
            panel[s, g] = jnp.zeros((256, 128), F32)

    stores = []
    for half in range(2):
        base = (odd if half == 0 else 1 - odd) * 8
        for c in range(half * n_gx, (half + 1) * n_gx):
            table, k, _ = chunks[c]
            loads[c].wait()
            count = table[k, 0, COUNT]

            @pl.loop(0, (count + STEP - 1) // STEP)
            def _(b):
                for u in range(STEP):
                    n = b * STEP + u
                    tag = table[k, 0, n]
                    valid = n < count
                    group = jnp.where(valid, base + ((tag >> 6) & 7), 16)
                    slot = jnp.where(valid, tag & 7, 0)
                    panel[slot, group, pl.ds((tag >> 3) & 7, 32, 8), :] = stage[c, n]

        for s in range(SLOTS):
            part = pl.ds(base, 8)
            store = pltpu.make_async_copy(
                panel.at[s, part], out.at[s, part], osems.at[half, s]
            )
            store.start()
            stores.append(store)
    for store in stores:
        store.wait()


def unpack(n_gx, tags, got_tags, pair_tags, bucket, got, pair):
    return pl.pallas_call(
        functools.partial(unpack_kernel, n_gx),
        out_shape=jax.ShapeDtypeStruct((SLOTS, 16, 256, 128), F32),
        in_specs=[SMEM] * 3 + [ANY] * 3,
        out_specs=ANY,
        scratch_shapes=[
            pltpu.VMEM((2 * n_gx, CAP + 2, 32, 128), F32),
            pltpu.VMEM((SLOTS, 17, 256, 128), F32),
            pltpu.SemaphoreType.DMA((2 * n_gx,)),
            pltpu.SemaphoreType.DMA((2, SLOTS)),
        ],
        compiler_params=pltpu.CompilerParams(vmem_limit_bytes=60 << 20),
        name="unpack",
    )(tags, got_tags, pair_tags, bucket, got, pair)


def body(blocks, prolong, columns, aggregate, column_slot, owner_row):
    n_gx, n_gy = lax.axis_size("gx"), lax.axis_size("gy")
    flat = blocks.reshape(NB, NNZ, 32, 128).transpose(0, 2, 1, 3).reshape(NB, 128, 128)
    q = prolong.reshape(16, 8, 32, 128).transpose(0, 2, 1, 3).reshape(16, 256, 128)
    ints = (columns.T, column_slot.T, aggregate.reshape(1, NB))
    nblocks, nright, nleft, *near = halo(n_gx, n_gy, flat, q, *ints)
    bucket, meta = coarse_buckets(n_gx, n_gy, owner_row, flat, nblocks, q, nright, nleft, ints, near)
    got, got_meta, pair, pair_meta = route(n_gx, bucket, meta)
    out = unpack(n_gx, meta, got_meta, pair_meta, bucket, got, pair)
    out = out.reshape(SLOTS, 16, 32, 8, 128).transpose(1, 3, 0, 2, 4)
    return out.reshape(NB, SLOTS, BS * BS)


def solution(mesh):
    placed = (
        P(("gx", "gy"), None, None),
        P(("gx", "gy"), None),
        P(("gx", "gy"), None),
        P(("gx", "gy")),
        P(("gx", "gy"), None),
        P(("gx", "gy")),
    )
    return jax.shard_map(
        body, mesh=mesh, in_specs=placed, out_specs=P(("gx", "gy"), None, None), check_vma=False
    )
```

```python
import functools

import jax
import jax.numpy as jnp
from jax import lax
from jax.experimental import pallas as pl
from jax.experimental.pallas import tpu as pltpu
from jax.sharding import PartitionSpec as P

BS = 64
NNZ = 4
SLOTS = 7
MESH = pl.DeviceIdType.MESH
ANY = pl.BlockSpec(memory_space=pl.ANY)
SMEM = pl.BlockSpec(memory_space=pltpu.SMEM)
VMEM = pl.BlockSpec(memory_space=pltpu.VMEM)

ROW_CAP = 9
ROW_BLOCKS = 6
CAP = ROW_CAP * ROW_BLOCKS
META = 128
NB = 128
NC = 64
EXT = NB + 6
F32 = jnp.float32
BF16 = jnp.bfloat16


def split(x):
    hi = x.astype(BF16)
    return hi, (x - hi.astype(F32)).astype(BF16)


def halo_kernel(n_gx, n_gy, *refs):
    n = len(refs) // 2
    sources, (send, recv) = refs[: n - 1], refs[-2:]
    targets = refs[n - 1 : -2]
    me = lax.axis_index("gx") * n_gy + lax.axis_index("gy")
    total = n_gx * n_gy
    up = lax.rem(me + 1, total)
    down = lax.rem(me + total - 1, total)
    up = (up // n_gy, lax.rem(up, n_gy))
    down = (down // n_gy, lax.rem(down, n_gy))
    blocks, prolong, columns, slots, aggregate = sources
    nblocks, nright, nleft, ncolumns, nslots, naggregate = targets
    barrier = pltpu.get_barrier_semaphore()
    for other in (up, down):
        pl.semaphore_signal(barrier, inc=1, device_id=other, device_id_type=MESH)
    pl.semaphore_wait(barrier, 2)
    copies = []
    plan = (
        (columns, ncolumns, down),
        (slots, nslots, down),
        (aggregate, naggregate, down),
        (prolong.at[15], nleft, up),
        (prolong.at[0], nright, down),
        (blocks.at[pl.ds(0, 2)], nblocks, down),
    )
    for n, (src, dst, to) in enumerate(plan):
        copy = pltpu.make_async_remote_copy(
            src_ref=src,
            dst_ref=dst,
            send_sem=send.at[n],
            recv_sem=recv.at[n],
            device_id=to,
            device_id_type=MESH,
        )
        copy.start()
        copies.append(copy)
    for copy in copies:
        copy.wait()


def halo(n_gx, n_gy, blocks, prolong, columns, slots, aggregate):
    return pl.pallas_call(
        functools.partial(halo_kernel, n_gx, n_gy),
        out_shape=(
            jax.ShapeDtypeStruct((2, 128, 128), F32),
            jax.ShapeDtypeStruct((256, 128), F32),
            jax.ShapeDtypeStruct((256, 128), F32),
            jax.ShapeDtypeStruct((NNZ, 128), jnp.int32),
            jax.ShapeDtypeStruct((NNZ, 128), jnp.int32),
            jax.ShapeDtypeStruct((1, 128), jnp.int32),
        ),
        in_specs=[ANY] * 5,
        out_specs=[ANY] * 6,
        scratch_shapes=[pltpu.SemaphoreType.DMA((6,)), pltpu.SemaphoreType.DMA((6,))],
        compiler_params=pltpu.CompilerParams(collective_id=0, has_side_effects=True),
        name="halo",
    )(blocks, prolong, columns, slots, aggregate)


PIECES = 8
COUNT = META - 1


def coarse_kernel(
    n_gx, n_gy, owner, blocks_hbm, nblocks, prolong, nright, nleft, own_ints, near_ints, bucket, meta,
    blocks, column, slot, parity, natural, weights, rows, lefts, sums, cnt, sems, isems,
):
    first = (lax.axis_index("gx") * n_gy + lax.axis_index("gy")) * NB
    fine = n_gx * n_gy * NB
    per = NB // PIECES
    for n, (table, own, near) in enumerate(zip((column, slot, parity), own_ints, near_ints)):
        pltpu.make_async_copy(own, table.at[0], isems.at[n, 0]).start()
        pltpu.make_async_copy(near, table.at[1], isems.at[n, 1]).start()

    def piece(n):
        part = pl.ds(n * per, per)
        return pltpu.make_async_copy(blocks_hbm.at[part], blocks.at[part], sems.at[n])

    last = pltpu.make_async_copy(nblocks, blocks.at[pl.ds(NB, 2)], sems.at[PIECES])
    for n in range(PIECES):
        piece(n).start()
    last.start()

    for d in range(n_gx):
        cnt[d] = 0
    low = lax.broadcasted_iota(jnp.int32, (32, 128), 1) < BS

    def prepare(x, flat):
        turned = pltpu.roll(flat, BS, 1)
        zero = jnp.zeros_like(flat)
        natural[0, pl.ds(0, 32, 2), :] = jnp.where(low, flat, zero)
        natural[0, pl.ds(1, 32, 2), :] = jnp.where(low, turned, zero)
        natural[1, pl.ds(0, 32, 2), :] = jnp.where(low, zero, turned)
        natural[1, pl.ds(1, 32, 2), :] = jnp.where(low, zero, flat)
        for side in range(2):
            hi, lo = split(natural[side])
            weights[x, side, 0] = hi
            weights[x, side, 1] = lo
        hi, lo = split(jnp.concatenate([flat[:, :BS], turned[:, :BS]], axis=0))
        rows[x] = jnp.concatenate([hi, lo, hi], axis=0)

    prepare(0, nleft[pl.ds(7, 32, 8), :])
    for r in range(5):
        prepare(NB + 1 + r, nright[pl.ds(r, 32, 8), :])

    @pl.loop(0, NB // 4)
    def _(g):
        for r in range(4):
            prepare(g * 4 + r + 1, prolong[g // 2, pl.ds(lax.rem(g, 2) * 4 + r, 32, 8), :])

    for n, (table, own, near) in enumerate(zip((column, slot, parity), own_ints, near_ints)):
        pltpu.make_async_copy(own, table.at[0], isems.at[n, 0]).wait()
        pltpu.make_async_copy(near, table.at[1], isems.at[n, 1]).wait()

    def at_row(table, i, k):
        return table[i // 128, k, lax.rem(i, 128)]

    def first_product(p):
        for t in range(4):
            i = p * 4 + t + 2
            parts = [blocks[i, pl.ds(k, 32, 4), :] for k in range(NNZ)]
            turned = [pltpu.roll(part, BS, 1) for part in parts]
            top = [jnp.where(low, parts[k], turned[k + 1]) for k in (0, 2)]
            bottom = [jnp.where(low, turned[k], parts[k + 1]) for k in (0, 2)]
            hi, lo = split(
                jnp.concatenate([jnp.concatenate(top, axis=1), jnp.concatenate(bottom, axis=1)], axis=0)
            )
            left = lax.dot_general(
                rows[i + 1],
                jnp.concatenate([hi, hi, lo], axis=0),
                (((0,), (0,)), ((), ())),
                preferred_element_type=F32,
            )
            hi, lo = split(left)
            for h in range(2):
                lanes = slice(h * 128, h * 128 + 128)
                lefts[t, h, :, :128] = hi[:, lanes]
                lefts[t, h, :, 128:] = lo[:, lanes]

    def second_product(p):
        values = []
        for t in range(4):
            i = p * 4 + t + 2
            for h in range(2):
                a, b = [
                    jnp.remainder(at_row(column, i, k) - first + 1, fine) for k in (2 * h, 2 * h + 1)
                ]
                both = jnp.concatenate(
                    [
                        jnp.concatenate([weights[a, 0, 0], weights[b, 1, 0]], axis=0),
                        jnp.concatenate([weights[a, 0, 1], weights[b, 1, 1]], axis=0),
                    ],
                    axis=1,
                )
                value = jnp.dot(
                    lefts[t, h], jnp.concatenate([both, both], axis=0), preferred_element_type=F32
                )
                values.append(value[:, :128] + value[:, 128:])
        return values

    def add_up(p, values):
        sums[...] = jnp.zeros_like(sums)
        mask = 0
        for t in range(4):
            i = p * 4 + t + 2
            second = lax.rem(at_row(parity, i, 0), 2) * SLOTS
            for k in range(NNZ):
                code = second + at_row(slot, i, k)
                mask = mask | (1 << code)
                lanes = slice(0, BS) if k % 2 == 0 else slice(BS, 128)
                sums[code, :, lanes] = sums[code, :, lanes] + values[t * 2 + k // 2][:, lanes]
        return mask

    def flush(p, mask):
        for r in range(2):
            row = owner[jnp.maximum(p * 2 + r, 0)]
            dest = row // (NC * n_gy)
            tag = lax.rem(row, NC) * 8
            start = cnt[dest]
            for s in range(SLOTS):
                c = r * SLOTS + s
                used = (mask >> c) & 1
                meta[dest, 0, start] = tag + s
                place = jnp.where(used == 1, start, CAP)
                start = start + used
                even = sums[c, pl.ds(0, 32, 2), :]
                odd = sums[c, pl.ds(1, 32, 2), :]
                bucket[dest, place] = jnp.where(low, even, pltpu.roll(odd, BS, 1)) + jnp.where(
                    low, pltpu.roll(even, BS, 1), odd
                )
            cnt[dest] = start

    piece(0).wait()
    first_product(0)

    def group(g, mask):
        @pl.when(g < PIECES - 1)
        def _():
            piece(g + 1).wait()

        @pl.when(g == PIECES - 1)
        def _():
            last.wait()

        def step(q, mask):
            p = g * 4 + q
            flush(p - 1, mask)
            values = second_product(p)
            mask = add_up(p, values)
            first_product(jnp.minimum(p + 1, NC // 2 - 1))
            return mask

        return lax.fori_loop(0, 4, step, mask)

    mask = lax.fori_loop(0, PIECES, group, jnp.int32(0))
    flush(NC // 2 - 1, mask)

    for d in range(n_gx):
        meta[d, 0, COUNT] = cnt[d]


def coarse_buckets(n_gx, n_gy, owner, blocks, nblocks, prolong, nright, nleft, own_ints, near_ints):
    def kernel(owner, blocks, nblocks, prolong, nright, nleft, c0, s0, a0, c1, s1, a1, *rest):
        coarse_kernel(
            n_gx, n_gy, owner, blocks, nblocks, prolong, nright, nleft, (c0, s0, a0), (c1, s1, a1), *rest
        )

    return pl.pallas_call(
        kernel,
        out_shape=(
            jax.ShapeDtypeStruct((n_gx, CAP + 2, 32, 128), F32),
            jax.ShapeDtypeStruct((n_gx, 1, META), jnp.int32),
        ),
        in_specs=[SMEM, ANY, ANY] + [VMEM] * 3 + [ANY] * 6,
        out_specs=(VMEM, SMEM),
        scratch_shapes=[
            pltpu.VMEM((NB + 2, 128, 128), F32),
            pltpu.SMEM((2, NNZ, 128), jnp.int32),
            pltpu.SMEM((2, NNZ, 128), jnp.int32),
            pltpu.SMEM((2, 1, 128), jnp.int32),
            pltpu.VMEM((2, BS, 128), F32),
            pltpu.VMEM((EXT, 2, 2, BS, 128), BF16),
            pltpu.VMEM((EXT, 3 * BS, BS), BF16),
            pltpu.VMEM((4, 2, BS, 256), BF16),
            pltpu.VMEM((2 * SLOTS, BS, 128), F32),
            pltpu.SMEM((n_gx,), jnp.int32),
            pltpu.SemaphoreType.DMA((PIECES + 1,)),
            pltpu.SemaphoreType.DMA((3, 2)),
        ],
        compiler_params=pltpu.CompilerParams(vmem_limit_bytes=56 << 20),
        name="coarse",
    )(owner, blocks, nblocks, prolong, nright, nleft, *own_ints, *near_ints)


ORDER = (1, 2, 6, 3, 7, 4, 5)


def flipped(index, k, bits):
    out = 0
    for b in range(bits):
        bit = lax.rem(index // (1 << b), 2)
        out = out + ((1 - bit) if (k >> b) & 1 else bit) * (1 << b)
    return out


def push(src, dst, send, recv, to):
    return pltpu.make_async_remote_copy(
        src_ref=src, dst_ref=dst, send_sem=send, recv_sem=recv, device_id=to, device_id_type=MESH
    )


def greet(others):
    barrier = pltpu.get_barrier_semaphore()
    for other in others:
        pl.semaphore_signal(barrier, inc=1, device_id=other, device_id_type=MESH)
    pl.semaphore_wait(barrier, len(others))


def route_kernel(bucket, meta, got, got_meta, pair, pair_meta, xs, xr, xms, xmr, zs, zr, zms, zmr):
    gx, gy = lax.axis_index("gx"), lax.axis_index("gy")
    n_gx = bucket.shape[0]
    partner = (gx, flipped(gy, 1, 4))
    peer = [None] + [flipped(gx, k, 3) for k in range(1, n_gx)]
    greet([(peer[k], gy) for k in range(1, n_gx)] + [partner])

    def forward(k, src, src_meta):
        made = [
            push(src_meta, pair_meta.at[k], zms.at[k], zmr.at[k], partner),
            push(src, pair.at[k], zs.at[k], zr.at[k], partner),
        ]
        for c in made:
            c.start()
        return made

    onward = forward(0, bucket.at[gx, pl.ds(0, CAP)], meta.at[gx])
    sent = {}
    for k in ORDER:
        to = (peer[k], gy)
        sent[k] = (
            push(meta.at[peer[k]], got_meta.at[k - 1], xms.at[k - 1], xmr.at[k - 1], to),
            push(bucket.at[peer[k], pl.ds(0, CAP)], got.at[k - 1], xs.at[k - 1], xr.at[k - 1], to),
        )
        for c in sent[k]:
            c.start()
    for k in ORDER:
        for c in sent[k]:
            c.wait_recv()
        onward += forward(k, got.at[k - 1], got_meta.at[k - 1])
    for k in ORDER:
        for c in sent[k]:
            c.wait_send()
    for c in onward:
        c.wait()


def route(n_gx, bucket, meta):
    data = lambda n: jax.ShapeDtypeStruct((n, CAP, 32, 128), F32)
    tags = lambda n: jax.ShapeDtypeStruct((n, 1, META), jnp.int32)
    sems = lambda n: pltpu.SemaphoreType.DMA((n,))
    return pl.pallas_call(
        route_kernel,
        out_shape=(data(n_gx - 1), tags(n_gx - 1), data(n_gx), tags(n_gx)),
        in_specs=[ANY] * 2,
        out_specs=[ANY] * 4,
        scratch_shapes=[sems(n_gx - 1)] * 4 + [sems(n_gx)] * 4,
        compiler_params=pltpu.CompilerParams(collective_id=1, has_side_effects=True),
        name="route",
    )(bucket, meta)


LEAN = 44
HEAD = 33
TAIL = LEAN - HEAD
EXTRA = 16
VOTES = 7


def lean_kernel(
    bucket, meta, got, got_meta, pair, pair_meta, extra, over,
    tails, tags, spare, ballots, heard, xs, xr, xms, xmr, zs, zr, zms, zmr, es, er, vs, vr, ls, ms,
):
    gx, gy = lax.axis_index("gx"), lax.axis_index("gy")
    n_gx = bucket.shape[0]
    partner = (gx, flipped(gy, 1, 4))
    peer = [gx] + [flipped(gx, k, 3) for k in range(1, n_gx)]
    voters = [partner] + [(gx, flipped(gy, k, 4)) for k in (2, 4, 8)] + [(peer[k], gy) for k in (1, 2, 4)]
    greet([(peer[k], gy) for k in range(1, n_gx)] + voters[:4])

    sent_meta = {}
    for k in ORDER:
        sent_meta[k] = push(
            meta.at[peer[k]], got_meta.at[k - 1], xms.at[k - 1], xmr.at[k - 1], (peer[k], gy)
        )
        sent_meta[k].start()
    sent = {}
    for k in ORDER:
        sent[k] = push(
            bucket.at[peer[k], pl.ds(0, LEAN)], got.at[k - 1], xs.at[k - 1], xr.at[k - 1], (peer[k], gy)
        )

    onward = []

    def forward(k, src, src_meta):
        made = [
            push(src_meta, pair_meta.at[k], zms.at[k], zmr.at[k], partner),
            push(src, pair.at[k], zs.at[k], zr.at[k], partner),
        ]
        for c in made:
            c.start()
        onward.extend(made)

    local = []

    def keep_tail(k, src):
        c = pltpu.make_async_copy(src, tails.at[k], ls.at[k])
        c.start()
        local.append(c)

    def keep_tags(k, src):
        c = pltpu.make_async_copy(src, tags.at[k], ms.at[k])
        c.start()
        c.wait()

    sent[ORDER[0]].start()
    forward(0, bucket.at[gx, pl.ds(0, HEAD)], meta.at[gx])
    for k in ORDER[1:]:
        sent[k].start()
    keep_tail(0, bucket.at[gx, pl.ds(HEAD, TAIL)])
    keep_tags(0, meta.at[gx])
    for k in ORDER:
        sent_meta[k].wait_recv()
        keep_tags(k, got_meta.at[k - 1])
    counts = [tags[k, 0, COUNT] for k in range(n_gx)]
    beyond = [jnp.maximum(n - HEAD, 0) for n in counts]
    starts = [0]
    for n in beyond:
        starts.append(starts[-1] + n)
    bad = jnp.where(starts[-1] > EXTRA, 1, 0)
    for n in counts:
        bad = jnp.maximum(bad, jnp.where(n > LEAN, 1, 0))
    ballots[0] = jnp.zeros((8, 128), jnp.int32) + bad

    votes = []

    def vote(n):
        c = push(ballots.at[n], heard.at[n], vs.at[n], vr.at[n], voters[n])
        c.start()
        votes.append(c)

    def count(n):
        votes[n].wait_recv()
        ballots[n + 1] = jnp.maximum(ballots[n], heard[n])

    for n, k in enumerate(ORDER):
        sent[k].wait_recv()
        forward(k, got.at[k - 1, pl.ds(0, HEAD)], got_meta.at[k - 1])
        keep_tail(k, got.at[k - 1, pl.ds(HEAD, TAIL)])
        if n > 0:
            count(n - 1)
        vote(n)
    for c in local:
        c.wait()
    for p in range(EXTRA):
        k, n = 0, p
        for j in range(1, n_gx):
            past = p >= starts[j]
            k = jnp.where(past, j, k)
            n = jnp.where(past, p - starts[j], n)
        spare[p] = tails[k, jnp.minimum(n, TAIL - 1)]
    count(VOTES - 1)
    rest = push(spare, extra, es, er, partner)
    rest.start()
    out = pltpu.make_async_copy(ballots.at[VOTES], over, ms.at[0])
    out.start()
    for k in ORDER:
        sent_meta[k].wait_send()
        sent[k].wait_send()
    for c in votes:
        c.wait_send()
    out.wait()
    for c in onward:
        c.wait()
    rest.wait()


def lean_route(n_gx, bucket, meta):
    data = lambda n, cap: jax.ShapeDtypeStruct((n, cap, 32, 128), F32)
    tags = lambda n: jax.ShapeDtypeStruct((n, 1, META), jnp.int32)
    sems = lambda *n: pltpu.SemaphoreType.DMA(n)
    return pl.pallas_call(
        lean_kernel,
        out_shape=(
            data(n_gx - 1, LEAN),
            tags(n_gx - 1),
            data(n_gx, HEAD),
            tags(n_gx),
            jax.ShapeDtypeStruct((EXTRA, 32, 128), F32),
            jax.ShapeDtypeStruct((8, 128), jnp.int32),
        ),
        in_specs=[ANY] * 2,
        out_specs=[ANY] * 6,
        scratch_shapes=[
            pltpu.VMEM((n_gx, TAIL, 32, 128), F32),
            pltpu.SMEM((n_gx, 1, META), jnp.int32),
            pltpu.VMEM((EXTRA, 32, 128), F32),
            pltpu.VMEM((VOTES + 1, 8, 128), jnp.int32),
            pltpu.VMEM((VOTES, 8, 128), jnp.int32),
        ]
        + [sems(n_gx - 1)] * 4
        + [sems(n_gx)] * 4
        + [sems(), sems(), sems(VOTES), sems(VOTES), sems(n_gx), sems(n_gx)],
        compiler_params=pltpu.CompilerParams(collective_id=2, has_side_effects=True),
        name="lean_route",
    )(bucket, meta)


STEP = 4


def unpack_kernel(n_gx, lean, tags, got_tags, pair_tags, bucket, got, pair, extra, out, *rest):
    mine, theirs, more, panel, sems, osems = rest
    gx, odd = lax.axis_index("gx"), lax.rem(lax.axis_index("gy"), 2)
    own_cap, pair_cap = got.shape[1], pair.shape[1]
    chunks = [(tags, gx, bucket.at[gx, pl.ds(0, own_cap)], mine.at[0, pl.ds(0, own_cap)])]
    chunks += [(got_tags, k, got.at[k], mine.at[k + 1, pl.ds(0, own_cap)]) for k in range(n_gx - 1)]
    chunks += [(pair_tags, k, pair.at[k], theirs.at[k, pl.ds(0, pair_cap)]) for k in range(n_gx)]
    loads = [
        pltpu.make_async_copy(source, target, sems.at[c])
        for c, (_, _, source, target) in enumerate(chunks)
    ]
    loads.append(pltpu.make_async_copy(extra, more, sems.at[2 * n_gx]))
    for load in loads:
        load.start()

    @pl.loop(0, 16)
    def _(g):
        for s in range(SLOTS):
            panel[s, g] = jnp.zeros((256, 128), F32)

    def place(base, tag, valid, block):
        group = jnp.where(valid, base + ((tag >> 6) & 7), 16)
        slot = jnp.where(valid, tag & 7, 0)
        panel[slot, group, pl.ds((tag >> 3) & 7, 32, 8), :] = block

    stores = []
    for half in range(2):
        base = (odd if half == 0 else 1 - odd) * 8
        cap = own_cap if half == 0 else pair_cap
        for c in range(n_gx):
            table, k, _, _ = chunks[half * n_gx + c]
            stage = (mine, theirs)[half]
            loads[half * n_gx + c].wait()
            count = jnp.minimum(table[k, 0, COUNT], cap)

            @pl.loop(0, (count + STEP - 1) // STEP)
            def _(b):
                for u in range(STEP):
                    n = b * STEP + u
                    place(base, table[k, 0, n], n < count, stage[c, n])

        if half == 1:
            loads[2 * n_gx].wait()
            if lean:
                at = 0
                for k in range(n_gx):
                    beyond = jnp.maximum(pair_tags[k, 0, COUNT] - pair_cap, 0)
                    begin = at

                    @pl.loop(0, beyond)
                    def _(n):
                        place(base, pair_tags[k, 0, pair_cap + n], True, more[begin + n])

                    at = at + beyond

        for s in range(SLOTS):
            part = pl.ds(base, 8)
            store = pltpu.make_async_copy(
                panel.at[s, part], out.at[s, part], osems.at[half, s]
            )
            store.start()
            stores.append(store)
    for store in stores:
        store.wait()


def unpack(n_gx, lean, tags, got_tags, pair_tags, bucket, got, pair, extra):
    return pl.pallas_call(
        functools.partial(unpack_kernel, n_gx, lean),
        out_shape=jax.ShapeDtypeStruct((SLOTS, 16, 256, 128), F32),
        in_specs=[SMEM] * 3 + [ANY] * 4,
        out_specs=ANY,
        scratch_shapes=[
            pltpu.VMEM((n_gx, got.shape[1] + STEP, 32, 128), F32),
            pltpu.VMEM((n_gx, pair.shape[1] + STEP, 32, 128), F32),
            pltpu.VMEM((EXTRA, 32, 128), F32),
            pltpu.VMEM((SLOTS, 17, 256, 128), F32),
            pltpu.SemaphoreType.DMA((2 * n_gx + 1,)),
            pltpu.SemaphoreType.DMA((2, SLOTS)),
        ],
        compiler_params=pltpu.CompilerParams(vmem_limit_bytes=60 << 20),
        name="unpack_lean" if lean else "unpack_full",
    )(tags, got_tags, pair_tags, bucket, got, pair, extra)


def body(blocks, prolong, columns, aggregate, column_slot, owner_row):
    n_gx, n_gy = lax.axis_size("gx"), lax.axis_size("gy")
    flat = blocks.reshape(NB, NNZ, 32, 128).transpose(0, 2, 1, 3).reshape(NB, 128, 128)
    q = prolong.reshape(16, 8, 32, 128).transpose(0, 2, 1, 3).reshape(16, 256, 128)
    ints = (columns.T, column_slot.T, aggregate.reshape(1, NB))
    nblocks, nright, nleft, *near = halo(n_gx, n_gy, flat, q, *ints)
    bucket, meta = coarse_buckets(n_gx, n_gy, owner_row, flat, nblocks, q, nright, nleft, ints, near)
    got, got_meta, pair, pair_meta, extra, over = lean_route(n_gx, bucket, meta)

    def full(_):
        got, got_meta, pair, pair_meta = route(n_gx, bucket, meta)
        return unpack(n_gx, False, meta, got_meta, pair_meta, bucket, got, pair, extra)

    def fitted(_):
        return unpack(n_gx, True, meta, got_meta, pair_meta, bucket, got, pair, extra)

    out = lax.cond(over[0, 0] > 0, full, fitted, 0)
    out = out.reshape(SLOTS, 16, 32, 8, 128).transpose(1, 3, 0, 2, 4)
    return out.reshape(NB, SLOTS, BS * BS)


def solution(mesh):
    placed = (
        P(("gx", "gy"), None, None),
        P(("gx", "gy"), None),
        P(("gx", "gy"), None),
        P(("gx", "gy")),
        P(("gx", "gy"), None),
        P(("gx", "gy")),
    )
    return jax.shard_map(
        body, mesh=mesh, in_specs=placed, out_specs=P(("gx", "gy"), None, None), check_vma=False
    )
```

```python
import functools

import jax
import jax.numpy as jnp
from jax import lax
from jax.experimental import pallas as pl
from jax.experimental.pallas import tpu as pltpu
from jax.sharding import PartitionSpec as P

BS = 64
NNZ = 4
SLOTS = 7
MESH = pl.DeviceIdType.MESH
ANY = pl.BlockSpec(memory_space=pl.ANY)
HBM = pl.BlockSpec(memory_space=pltpu.HBM)
SMEM = pl.BlockSpec(memory_space=pltpu.SMEM)
VMEM = pl.BlockSpec(memory_space=pltpu.VMEM)

ROW_CAP = 9
ROW_BLOCKS = 6
CAP = ROW_CAP * ROW_BLOCKS
META = 128
NB = 128
NC = 64
EXT = NB + 6
F32 = jnp.float32
BF16 = jnp.bfloat16


def split(x):
    hi = x.astype(BF16)
    return hi, (x - hi.astype(F32)).astype(BF16)


def halo_kernel(n_gx, n_gy, *refs):
    n = len(refs) // 2
    sources, (send, recv) = refs[: n - 1], refs[-2:]
    targets = refs[n - 1 : -2]
    me = lax.axis_index("gx") * n_gy + lax.axis_index("gy")
    total = n_gx * n_gy
    up = lax.rem(me + 1, total)
    down = lax.rem(me + total - 1, total)
    up = (up // n_gy, lax.rem(up, n_gy))
    down = (down // n_gy, lax.rem(down, n_gy))
    blocks, prolong, columns, slots, aggregate = sources
    nblocks, nright, nleft, ncolumns, nslots, naggregate = targets
    barrier = pltpu.get_barrier_semaphore()
    for other in (up, down):
        pl.semaphore_signal(barrier, inc=1, device_id=other, device_id_type=MESH)
    pl.semaphore_wait(barrier, 2)
    copies = []
    plan = (
        (columns, ncolumns, down),
        (slots, nslots, down),
        (aggregate, naggregate, down),
        (prolong.at[15, :, pl.ds(7, 1)], nleft, up),
        (prolong.at[0, :, pl.ds(0, 5)], nright, down),
        (blocks.at[pl.ds(0, 2)], nblocks, down),
    )
    for n, (src, dst, to) in enumerate(plan):
        copy = pltpu.make_async_remote_copy(
            src_ref=src,
            dst_ref=dst,
            send_sem=send.at[n],
            recv_sem=recv.at[n],
            device_id=to,
            device_id_type=MESH,
        )
        copy.start()
        copies.append(copy)
    for copy in copies:
        copy.wait()


def halo(n_gx, n_gy, blocks, prolong, columns, slots, aggregate):
    return pl.pallas_call(
        functools.partial(halo_kernel, n_gx, n_gy),
        out_shape=(
            jax.ShapeDtypeStruct((2, 128, 128), F32),
            jax.ShapeDtypeStruct((32, 5, 128), F32),
            jax.ShapeDtypeStruct((32, 1, 128), F32),
            jax.ShapeDtypeStruct((NNZ, 128), jnp.int32),
            jax.ShapeDtypeStruct((NNZ, 128), jnp.int32),
            jax.ShapeDtypeStruct((1, 128), jnp.int32),
        ),
        in_specs=[HBM] * 5,
        out_specs=[ANY] * 6,
        scratch_shapes=[pltpu.SemaphoreType.DMA((6,)), pltpu.SemaphoreType.DMA((6,))],
        compiler_params=pltpu.CompilerParams(collective_id=0, has_side_effects=True, vmem_limit_bytes=1 << 20),
        name="halo",
    )(*(pltpu.with_memory_space_constraint(x, pltpu.HBM) for x in (blocks, prolong, columns, slots, aggregate)))


COUNT = META - 1


def coarse_kernel(
    n_gx, n_gy, owner, blocks, nblocks, prolong, nright, nleft, own_ints, near_ints, bucket, meta,
    column, slot, parity, natural, weights, rows, lefts, sums, cnt, isems,
):
    first = (lax.axis_index("gx") * n_gy + lax.axis_index("gy")) * NB
    fine = n_gx * n_gy * NB
    shift = (NC * n_gy).bit_length() - 1
    for n, (table, own, near) in enumerate(zip((column, slot, parity), own_ints, near_ints)):
        pltpu.make_async_copy(own, table.at[0], isems.at[n, 0]).start()
        pltpu.make_async_copy(near, table.at[1], isems.at[n, 1]).start()

    for d in range(n_gx):
        cnt[d] = 0
    low = lax.broadcasted_iota(jnp.int32, (32, 128), 1) < BS

    def prepare(x, flat):
        turned = pltpu.roll(flat, BS, 1)
        zero = jnp.zeros_like(flat)
        natural[0, pl.ds(0, 32, 2), :] = jnp.where(low, flat, zero)
        natural[0, pl.ds(1, 32, 2), :] = jnp.where(low, turned, zero)
        natural[1, pl.ds(0, 32, 2), :] = jnp.where(low, zero, turned)
        natural[1, pl.ds(1, 32, 2), :] = jnp.where(low, zero, flat)
        for side in range(2):
            hi, lo = split(natural[side])
            weights[x, side, 0] = hi
            weights[x, side, 1] = lo
        hi, lo = split(jnp.concatenate([flat[:, :BS], turned[:, :BS]], axis=0))
        rows[x] = jnp.concatenate([hi, lo, hi], axis=0)

    prepare(0, nleft[:, 0, :])
    for r in range(5):
        prepare(NB + 1 + r, nright[:, r, :])

    @pl.loop(0, NB // 4)
    def _(g):
        for r in range(4):
            prepare(g * 4 + r + 1, prolong[g // 2, pl.ds(lax.rem(g, 2) * 4 + r, 32, 8), :])

    for n, (table, own, near) in enumerate(zip((column, slot, parity), own_ints, near_ints)):
        pltpu.make_async_copy(own, table.at[0], isems.at[n, 0]).wait()
        pltpu.make_async_copy(near, table.at[1], isems.at[n, 1]).wait()

    def at_row(table, i, k):
        return table[i >> 7, k, i & 127]

    def first_product(p, block_rows):
        for t in range(4):
            i = p * 4 + t + 2
            source, at = block_rows[t]
            parts = [source[at, pl.ds(k, 32, 4), :] for k in range(NNZ)]
            turned = [pltpu.roll(part, BS, 1) for part in parts]
            top = [jnp.where(low, parts[k], turned[k + 1]) for k in (0, 2)]
            bottom = [jnp.where(low, turned[k], parts[k + 1]) for k in (0, 2)]
            hi, lo = split(
                jnp.concatenate([jnp.concatenate(top, axis=1), jnp.concatenate(bottom, axis=1)], axis=0)
            )
            left = lax.dot_general(
                rows[i + 1],
                jnp.concatenate([hi, hi, lo], axis=0),
                (((0,), (0,)), ((), ())),
                preferred_element_type=F32,
            )
            hi, lo = split(left)
            for h in range(2):
                lanes = slice(h * 128, h * 128 + 128)
                lefts[t, h, :, :128] = hi[:, lanes]
                lefts[t, h, :, 128:] = lo[:, lanes]

    def second_product(p):
        values = []
        for t in range(4):
            i = p * 4 + t + 2
            for h in range(2):
                a, b = [
                    (at_row(column, i, k) - first + 1) & (fine - 1) for k in (2 * h, 2 * h + 1)
                ]
                both = jnp.concatenate(
                    [
                        jnp.concatenate([weights[a, 0, 0], weights[b, 1, 0]], axis=0),
                        jnp.concatenate([weights[a, 0, 1], weights[b, 1, 1]], axis=0),
                    ],
                    axis=1,
                )
                value = jnp.dot(
                    lefts[t, h], jnp.concatenate([both, both], axis=0), preferred_element_type=F32
                )
                values.append(value[:, :128] + value[:, 128:])
        return values

    def add_up(p, values):
        sums[...] = jnp.zeros_like(sums)
        mask = 0
        for t in range(4):
            i = p * 4 + t + 2
            second = (at_row(parity, i, 0) & 1) * SLOTS
            for k in range(NNZ):
                code = second + at_row(slot, i, k)
                mask = mask | (1 << code)
                lanes = slice(0, BS) if k % 2 == 0 else slice(BS, 128)
                sums[code, :, lanes] = sums[code, :, lanes] + values[t * 2 + k // 2][:, lanes]
        return mask

    def flush(p, mask):
        for r in range(2):
            row = owner[jnp.maximum(p * 2 + r, 0)]
            dest = row >> shift
            tag = (row & (NC - 1)) * 8
            start = cnt[dest]
            for s in range(SLOTS):
                c = r * SLOTS + s
                used = (mask >> c) & 1
                meta[dest, 0, start] = tag + s
                place = jnp.where(used == 1, start, CAP)
                start = start + used
                even = sums[c, pl.ds(0, 32, 2), :]
                odd = sums[c, pl.ds(1, 32, 2), :]
                bucket[dest, place] = jnp.where(low, even, pltpu.roll(odd, BS, 1)) + jnp.where(
                    low, pltpu.roll(even, BS, 1), odd
                )
            cnt[dest] = start

    def own(p):
        return [(blocks, p * 4 + t + 2) for t in range(4)]

    end = NC // 2 - 1

    def step(p, mask, upcoming):
        flush(p - 1, mask)
        values = second_product(p)
        mask = add_up(p, values)
        if upcoming is not None:
            first_product(p + 1, upcoming)
        return mask

    first_product(0, own(0))
    mask = lax.fori_loop(0, end - 1, lambda p, mask: step(p, mask, own(p + 1)), jnp.int32(0))
    mask = step(end - 1, mask, own(end)[:2] + [(nblocks, 0), (nblocks, 1)])
    mask = step(end, mask, None)
    flush(end, mask)

    for d in range(n_gx):
        meta[d, 0, COUNT] = cnt[d]


def coarse_buckets(n_gx, n_gy, owner, blocks, nblocks, prolong, nright, nleft, own_ints, near_ints):
    def kernel(owner, blocks, nblocks, prolong, nright, nleft, c0, s0, a0, c1, s1, a1, *rest):
        coarse_kernel(
            n_gx, n_gy, owner, blocks, nblocks, prolong, nright, nleft, (c0, s0, a0), (c1, s1, a1), *rest
        )

    return pl.pallas_call(
        kernel,
        out_shape=(
            jax.ShapeDtypeStruct((n_gx, CAP + 2, 32, 128), F32),
            jax.ShapeDtypeStruct((n_gx, 1, META), jnp.int32),
        ),
        in_specs=[SMEM] + [VMEM] * 5 + [ANY] * 6,
        out_specs=(VMEM, SMEM),
        scratch_shapes=[
            pltpu.SMEM((2, NNZ, 128), jnp.int32),
            pltpu.SMEM((2, NNZ, 128), jnp.int32),
            pltpu.SMEM((2, 1, 128), jnp.int32),
            pltpu.VMEM((2, BS, 128), F32),
            pltpu.VMEM((EXT, 2, 2, BS, 128), BF16),
            pltpu.VMEM((EXT, 3 * BS, BS), BF16),
            pltpu.VMEM((4, 2, BS, 256), BF16),
            pltpu.VMEM((2 * SLOTS, BS, 128), F32),
            pltpu.SMEM((n_gx,), jnp.int32),
            pltpu.SemaphoreType.DMA((3, 2)),
        ],
        compiler_params=pltpu.CompilerParams(vmem_limit_bytes=20 << 20),
        name="coarse",
    )(owner, blocks, nblocks, prolong, nright, nleft, *own_ints, *near_ints)


ORDER = (1, 2, 6, 3, 7, 4, 5)


def flipped(index, k, bits):
    out = 0
    for b in range(bits):
        bit = lax.rem(index // (1 << b), 2)
        out = out + ((1 - bit) if (k >> b) & 1 else bit) * (1 << b)
    return out


def push(src, dst, send, recv, to):
    return pltpu.make_async_remote_copy(
        src_ref=src, dst_ref=dst, send_sem=send, recv_sem=recv, device_id=to, device_id_type=MESH
    )


def greet(others):
    barrier = pltpu.get_barrier_semaphore()
    for other in others:
        pl.semaphore_signal(barrier, inc=1, device_id=other, device_id_type=MESH)
    pl.semaphore_wait(barrier, len(others))


def route_kernel(bucket, meta, got, got_meta, pair, pair_meta, xs, xr, xms, xmr, zs, zr, zms, zmr):
    gx, gy = lax.axis_index("gx"), lax.axis_index("gy")
    n_gx = bucket.shape[0]
    partner = (gx, flipped(gy, 1, 4))
    peer = [None] + [flipped(gx, k, 3) for k in range(1, n_gx)]
    greet([(peer[k], gy) for k in range(1, n_gx)] + [partner])

    def forward(k, src, src_meta):
        made = [
            push(src_meta, pair_meta.at[k], zms.at[k], zmr.at[k], partner),
            push(src, pair.at[k], zs.at[k], zr.at[k], partner),
        ]
        for c in made:
            c.start()
        return made

    onward = forward(0, bucket.at[gx, pl.ds(0, CAP)], meta.at[gx])
    sent = {}
    for k in ORDER:
        to = (peer[k], gy)
        sent[k] = (
            push(meta.at[peer[k]], got_meta.at[k - 1], xms.at[k - 1], xmr.at[k - 1], to),
            push(bucket.at[peer[k], pl.ds(0, CAP)], got.at[k - 1], xs.at[k - 1], xr.at[k - 1], to),
        )
        for c in sent[k]:
            c.start()
    for k in ORDER:
        for c in sent[k]:
            c.wait_recv()
        onward += forward(k, got.at[k - 1], got_meta.at[k - 1])
    for k in ORDER:
        for c in sent[k]:
            c.wait_send()
    for c in onward:
        c.wait()


def route(n_gx, bucket, meta):
    data = lambda n: jax.ShapeDtypeStruct((n, CAP, 32, 128), F32)
    tags = lambda n: jax.ShapeDtypeStruct((n, 1, META), jnp.int32)
    sems = lambda n: pltpu.SemaphoreType.DMA((n,))
    return pl.pallas_call(
        route_kernel,
        out_shape=(data(n_gx - 1), tags(n_gx - 1), data(n_gx), tags(n_gx)),
        in_specs=[ANY] * 2,
        out_specs=[ANY] * 4,
        scratch_shapes=[sems(n_gx - 1)] * 4 + [sems(n_gx)] * 4,
        compiler_params=pltpu.CompilerParams(collective_id=1, has_side_effects=True, vmem_limit_bytes=4 << 20),
        name="route",
    )(bucket, meta)


LEAN = 44
HEAD = 33
TAIL = LEAN - HEAD
EXTRA = 16
VOTES = 7


def lean_kernel(
    bucket, meta, got, got_meta, pair, pair_meta, extra, over,
    tags, spare, ballots, heard, result, xs, xr, xms, xmr, zs, zr, zms, zmr, es, er, vs, vr, ms,
):
    gx, gy = lax.axis_index("gx"), lax.axis_index("gy")
    n_gx = bucket.shape[0]
    partner = (gx, flipped(gy, 1, 4))
    peer = [gx] + [flipped(gx, k, 3) for k in range(1, n_gx)]
    voters = [partner] + [(gx, flipped(gy, k, 4)) for k in (2, 4, 8)] + [(peer[k], gy) for k in (1, 2, 4)]
    greet([(peer[k], gy) for k in range(1, n_gx)] + voters[:4])

    sent_meta = {}
    for k in ORDER:
        sent_meta[k] = push(
            meta.at[peer[k]], got_meta.at[k - 1], xms.at[k - 1], xmr.at[k - 1], (peer[k], gy)
        )
        sent_meta[k].start()
    sent = {}
    for k in ORDER:
        sent[k] = push(
            bucket.at[peer[k], pl.ds(0, LEAN)], got.at[k - 1], xs.at[k - 1], xr.at[k - 1], (peer[k], gy)
        )

    onward = []

    def forward(k, src, src_meta):
        made = [
            push(src_meta, pair_meta.at[k], zms.at[k], zmr.at[k], partner),
            push(src, pair.at[k], zs.at[k], zr.at[k], partner),
        ]
        for c in made:
            c.start()
        onward.extend(made)

    def keep_tags(k, src):
        c = pltpu.make_async_copy(src, tags.at[k], ms.at[k])
        c.start()
        c.wait()

    sent[ORDER[0]].start()
    forward(0, bucket.at[gx, pl.ds(0, HEAD)], meta.at[gx])
    for k in ORDER[1:]:
        sent[k].start()
    keep_tags(0, meta.at[gx])
    for k in ORDER:
        sent_meta[k].wait_recv()
        keep_tags(k, got_meta.at[k - 1])
    counts = [tags[k, 0, COUNT] for k in range(n_gx)]
    beyond = [jnp.maximum(n - HEAD, 0) for n in counts]
    starts = [0]
    for n in beyond:
        starts.append(starts[-1] + n)
    bad = jnp.where(starts[-1] > EXTRA, 1, 0)
    for n in counts:
        bad = jnp.maximum(bad, jnp.where(n > LEAN, 1, 0))
    ballots[0] = jnp.zeros((8, 128), jnp.int32) + bad

    votes = []

    def vote(n):
        c = push(ballots.at[n], heard.at[n], vs.at[n], vr.at[n], voters[n])
        c.start()
        votes.append(c)

    def count(n):
        votes[n].wait_recv()
        ballots[n + 1] = jnp.maximum(ballots[n], heard[n])

    for n, k in enumerate(ORDER):
        sent[k].wait_recv()
        forward(k, got.at[k - 1, pl.ds(0, HEAD)], got_meta.at[k - 1])
        if n > 0:
            count(n - 1)
        vote(n)
    for p in range(EXTRA):
        k, n = 0, p
        for j in range(1, n_gx):
            past = p >= starts[j]
            k = jnp.where(past, j, k)
            n = jnp.where(past, p - starts[j], n)
        at = HEAD + jnp.minimum(n, TAIL - 1)
        spare[p] = jnp.where(k == 0, bucket[gx, at], got[jnp.maximum(k, 1) - 1, at])
    count(VOTES - 1)
    rest = push(spare, extra, es, er, partner)
    rest.start()
    out = pltpu.make_async_copy(ballots.at[VOTES], result, ms.at[0])
    out.start()
    for k in ORDER:
        sent_meta[k].wait_send()
        sent[k].wait_send()
    for c in votes:
        c.wait_send()
    out.wait()
    over[0, 0] = result[0, 0]
    for c in onward:
        c.wait()
    rest.wait()


def lean_route(n_gx, bucket, meta):
    data = lambda n, cap: jax.ShapeDtypeStruct((n, cap, 32, 128), F32)
    tags = lambda n: jax.ShapeDtypeStruct((n, 1, META), jnp.int32)
    sems = lambda *n: pltpu.SemaphoreType.DMA(n)
    return pl.pallas_call(
        lean_kernel,
        out_shape=(
            data(n_gx - 1, LEAN),
            tags(n_gx - 1),
            data(n_gx, HEAD),
            tags(n_gx),
            jax.ShapeDtypeStruct((EXTRA, 32, 128), F32),
            jax.ShapeDtypeStruct((1, 1), jnp.int32),
        ),
        in_specs=[VMEM, ANY],
        out_specs=[VMEM] + [ANY] * 4 + [SMEM],
        scratch_shapes=[
            pltpu.SMEM((n_gx, 1, META), jnp.int32),
            pltpu.VMEM((EXTRA, 32, 128), F32),
            pltpu.VMEM((VOTES + 1, 8, 128), jnp.int32),
            pltpu.VMEM((VOTES, 8, 128), jnp.int32),
            pltpu.SMEM((8, 128), jnp.int32),
        ]
        + [sems(n_gx - 1)] * 4
        + [sems(n_gx)] * 4
        + [sems(), sems(), sems(VOTES), sems(VOTES), sems(n_gx)],
        compiler_params=pltpu.CompilerParams(collective_id=2, has_side_effects=True, vmem_limit_bytes=4 << 20),
        name="lean_route",
    )(bucket, meta)


STEP = 4


def unpack_kernel(n_gx, lean, tags, got_tags, pair_tags, bucket, got, pair, extra, out, *rest):
    panel, osems = rest
    gx, odd = lax.axis_index("gx"), lax.rem(lax.axis_index("gy"), 2)
    own_cap, pair_cap = got.shape[1], pair.shape[1]
    chunks = [(tags, gx, bucket, gx)]
    chunks += [(got_tags, k, got, k) for k in range(n_gx - 1)]
    chunks += [(pair_tags, k, pair, k) for k in range(n_gx)]

    @pl.loop(0, 16)
    def _(g):
        for s in range(SLOTS):
            panel[s, g] = jnp.zeros((256, 128), F32)

    def place(base, tag, valid, block):
        group = jnp.where(valid, base + ((tag >> 6) & 7), 16)
        slot = jnp.where(valid, tag & 7, 0)
        panel[slot, group, pl.ds((tag >> 3) & 7, 32, 8), :] = block

    stores = []
    for half in range(2):
        base = (odd if half == 0 else 1 - odd) * 8
        cap = own_cap if half == 0 else pair_cap
        for c in range(n_gx):
            table, k, stage, part = chunks[half * n_gx + c]
            count = jnp.minimum(table[k, 0, COUNT], cap)

            @pl.loop(0, (count + STEP - 1) // STEP)
            def _(b):
                for u in range(STEP):
                    n = b * STEP + u
                    place(base, table[k, 0, n], n < count, stage[part, jnp.minimum(n, cap - 1)])

        if half == 1:
            if lean:
                at = 0
                for k in range(n_gx):
                    beyond = jnp.maximum(pair_tags[k, 0, COUNT] - pair_cap, 0)
                    begin = at

                    @pl.loop(0, beyond)
                    def _(n):
                        place(base, pair_tags[k, 0, pair_cap + n], True, extra[begin + n])

                    at = at + beyond

        for s in range(SLOTS):
            part = pl.ds(base, 8)
            store = pltpu.make_async_copy(
                panel.at[s, part], out.at[s, part], osems.at[half, s]
            )
            store.start()
            stores.append(store)
    for store in stores:
        store.wait()


def unpack(n_gx, lean, tags, got_tags, pair_tags, bucket, got, pair, extra):
    return pl.pallas_call(
        functools.partial(unpack_kernel, n_gx, lean),
        out_shape=jax.ShapeDtypeStruct((SLOTS, 16, 256, 128), F32),
        in_specs=[SMEM] * 3 + [VMEM] * 4,
        out_specs=ANY,
        scratch_shapes=[
            pltpu.VMEM((SLOTS, 17, 256, 128), F32),
            pltpu.SemaphoreType.DMA((2, SLOTS)),
        ],
        compiler_params=pltpu.CompilerParams(vmem_limit_bytes=40 << 20),
        name="unpack_lean" if lean else "unpack_full",
    )(tags, got_tags, pair_tags, bucket, got, pair, extra)


def body(blocks, prolong, columns, aggregate, column_slot, owner_row):
    n_gx, n_gy = lax.axis_size("gx"), lax.axis_size("gy")
    flat = blocks.reshape(NB, NNZ, 32, 128).transpose(0, 2, 1, 3).reshape(NB, 128, 128)
    q = prolong.reshape(16, 8, 32, 128).transpose(0, 2, 1, 3).reshape(16, 256, 128)
    ints = (columns.T, column_slot.T, aggregate.reshape(1, NB))
    nblocks, nright, nleft, *near = halo(n_gx, n_gy, flat, q.reshape(16, 32, 8, 128), *ints)
    bucket, meta = coarse_buckets(n_gx, n_gy, owner_row, flat, nblocks, q, nright, nleft, ints, near)
    got, got_meta, pair, pair_meta, extra, over = lean_route(n_gx, bucket, meta)

    def full(_):
        got, got_meta, pair, pair_meta = route(n_gx, bucket, meta)
        return unpack(n_gx, False, meta, got_meta, pair_meta, bucket, got, pair, extra)

    def fitted(_):
        return unpack(n_gx, True, meta, got_meta, pair_meta, bucket, got, pair, extra)

    out = lax.cond(over[0, 0] > 0, full, fitted, 0)
    out = out.reshape(SLOTS, 16, 32, 8, 128).transpose(1, 3, 0, 2, 4)
    return out.reshape(NB, SLOTS, BS * BS)


def solution(mesh):
    placed = (
        P(("gx", "gy"), None, None),
        P(("gx", "gy"), None),
        P(("gx", "gy"), None),
        P(("gx", "gy")),
        P(("gx", "gy"), None),
        P(("gx", "gy")),
    )
    return jax.shard_map(
        body, mesh=mesh, in_specs=placed, out_specs=P(("gx", "gy"), None, None), check_vma=False
    )
```

```python
import functools

import jax
import jax.numpy as jnp
from jax import lax
from jax.experimental import pallas as pl
from jax.experimental.pallas import tpu as pltpu
from jax.sharding import PartitionSpec as P

BS = 64
NNZ = 4
SLOTS = 7
MESH = pl.DeviceIdType.MESH
ANY = pl.BlockSpec(memory_space=pl.ANY)
HBM = pl.BlockSpec(memory_space=pltpu.HBM)
SMEM = pl.BlockSpec(memory_space=pltpu.SMEM)
VMEM = pl.BlockSpec(memory_space=pltpu.VMEM)

ROW_CAP = 9
ROW_BLOCKS = 6
CAP = ROW_CAP * ROW_BLOCKS
META = 128
NB = 128
NC = 64
EXT = NB + 6
F32 = jnp.float32
BF16 = jnp.bfloat16


def split(x):
    hi = x.astype(BF16)
    return hi, (x - hi.astype(F32)).astype(BF16)


def prepare(weights, rows, natural, x, flat):
    low = lax.broadcasted_iota(jnp.int32, (32, 128), 1) < BS
    turned = pltpu.roll(flat, BS, 1)
    zero = jnp.zeros_like(flat)
    natural[0, pl.ds(0, 32, 2), :] = jnp.where(low, flat, zero)
    natural[0, pl.ds(1, 32, 2), :] = jnp.where(low, turned, zero)
    natural[1, pl.ds(0, 32, 2), :] = jnp.where(low, zero, turned)
    natural[1, pl.ds(1, 32, 2), :] = jnp.where(low, zero, flat)
    for side in range(2):
        hi, lo = split(natural[side])
        weights[x, side, 0] = hi
        weights[x, side, 1] = lo
    hi, lo = split(jnp.concatenate([flat[:, :BS], turned[:, :BS]], axis=0))
    rows[x] = jnp.concatenate([hi, lo, hi], axis=0)


def halo_kernel(
    n_gx, n_gy, blocks, prolong, columns, slots, aggregate,
    nblocks, ncolumns, nslots, naggregate, weights, rows, own, nright, nleft, natural, send, recv, sem,
):
    me = lax.axis_index("gx") * n_gy + lax.axis_index("gy")
    total = n_gx * n_gy
    up = lax.rem(me + 1, total)
    down = lax.rem(me + total - 1, total)
    up = (up // n_gy, lax.rem(up, n_gy))
    down = (down // n_gy, lax.rem(down, n_gy))
    fetch = pltpu.make_async_copy(prolong, own, sem)
    fetch.start()
    barrier = pltpu.get_barrier_semaphore()
    for other in (up, down):
        pl.semaphore_signal(barrier, inc=1, device_id=other, device_id_type=MESH)
    pl.semaphore_wait(barrier, 2)
    copies = []
    plan = (
        (columns, ncolumns, down),
        (slots, nslots, down),
        (aggregate, naggregate, down),
        (prolong.at[15, :, pl.ds(7, 1)], nleft, up),
        (prolong.at[0, :, pl.ds(0, 5)], nright, down),
        (blocks.at[pl.ds(0, 2)], nblocks, down),
    )
    for n, (src, dst, to) in enumerate(plan):
        copy = pltpu.make_async_remote_copy(
            src_ref=src,
            dst_ref=dst,
            send_sem=send.at[n],
            recv_sem=recv.at[n],
            device_id=to,
            device_id_type=MESH,
        )
        copy.start()
        copies.append(copy)
    fetch.wait()

    @pl.loop(0, 16)
    def _(g):
        for r in range(8):
            prepare(weights, rows, natural.at[r % 2], g * 8 + r + 1, own[g, :, r, :])

    for copy in copies:
        copy.wait()
    prepare(weights, rows, natural.at[0], 0, nleft[:, 0, :])
    for r in range(5):
        prepare(weights, rows, natural.at[1 - r % 2], NB + 1 + r, nright[:, r, :])


def halo(n_gx, n_gy, blocks, prolong, columns, slots, aggregate):
    return pl.pallas_call(
        functools.partial(halo_kernel, n_gx, n_gy),
        out_shape=(
            jax.ShapeDtypeStruct((2, 128, 128), F32),
            jax.ShapeDtypeStruct((NNZ, 128), jnp.int32),
            jax.ShapeDtypeStruct((NNZ, 128), jnp.int32),
            jax.ShapeDtypeStruct((1, 128), jnp.int32),
            jax.ShapeDtypeStruct((EXT, 2, 2, BS, 128), BF16),
            jax.ShapeDtypeStruct((EXT, 3 * BS, BS), BF16),
        ),
        in_specs=[HBM] * 5,
        out_specs=[ANY] * 4 + [VMEM] * 2,
        scratch_shapes=[
            pltpu.VMEM((16, 32, 8, 128), F32),
            pltpu.VMEM((32, 5, 128), F32),
            pltpu.VMEM((32, 1, 128), F32),
            pltpu.VMEM((2, 2, BS, 128), F32),
            pltpu.SemaphoreType.DMA((6,)),
            pltpu.SemaphoreType.DMA((6,)),
            pltpu.SemaphoreType.DMA(()),
        ],
        compiler_params=pltpu.CompilerParams(collective_id=0, has_side_effects=True, vmem_limit_bytes=4 << 20),
        name="halo",
    )(*(pltpu.with_memory_space_constraint(x, pltpu.HBM) for x in (blocks, prolong, columns, slots, aggregate)))


COUNT = META - 1


def coarse_kernel(
    n_gx, n_gy, owner, blocks, nblocks, weights, rows, own_ints, near_ints, bucket, meta,
    column, slot, parity, lefts, sums, cnt, isems,
):
    first = (lax.axis_index("gx") * n_gy + lax.axis_index("gy")) * NB
    fine = n_gx * n_gy * NB
    shift = (NC * n_gy).bit_length() - 1
    for n, (table, own, near) in enumerate(zip((column, slot, parity), own_ints, near_ints)):
        pltpu.make_async_copy(own, table.at[0], isems.at[n, 0]).start()
        pltpu.make_async_copy(near, table.at[1], isems.at[n, 1]).start()

    for d in range(n_gx):
        cnt[d] = 0
    low = lax.broadcasted_iota(jnp.int32, (32, 128), 1) < BS

    for n, (table, own, near) in enumerate(zip((column, slot, parity), own_ints, near_ints)):
        pltpu.make_async_copy(own, table.at[0], isems.at[n, 0]).wait()
        pltpu.make_async_copy(near, table.at[1], isems.at[n, 1]).wait()

    def at_row(table, i, k):
        return table[i >> 7, k, i & 127]

    def first_product(p, block_rows):
        for t in range(4):
            i = p * 4 + t + 2
            source, at = block_rows[t]
            parts = [source[at, pl.ds(k, 32, 4), :] for k in range(NNZ)]
            turned = [pltpu.roll(part, BS, 1) for part in parts]
            top = [jnp.where(low, parts[k], turned[k + 1]) for k in (0, 2)]
            bottom = [jnp.where(low, turned[k], parts[k + 1]) for k in (0, 2)]
            hi, lo = split(
                jnp.concatenate([jnp.concatenate(top, axis=1), jnp.concatenate(bottom, axis=1)], axis=0)
            )
            left = lax.dot_general(
                rows[i + 1],
                jnp.concatenate([hi, hi, lo], axis=0),
                (((0,), (0,)), ((), ())),
                preferred_element_type=F32,
            )
            hi, lo = split(left)
            for h in range(2):
                lanes = slice(h * 128, h * 128 + 128)
                lefts[t, h, :, :128] = hi[:, lanes]
                lefts[t, h, :, 128:] = lo[:, lanes]

    def second_product(p):
        sums[...] = jnp.zeros_like(sums)
        mask = 0
        for t in range(4):
            i = p * 4 + t + 2
            second = (at_row(parity, i, 0) & 1) * SLOTS
            for h in range(2):
                a, b = [
                    (at_row(column, i, k) - first + 1) & (fine - 1) for k in (2 * h, 2 * h + 1)
                ]
                both = jnp.concatenate(
                    [
                        jnp.concatenate([weights[a, 0, 0], weights[b, 1, 0]], axis=0),
                        jnp.concatenate([weights[a, 0, 1], weights[b, 1, 1]], axis=0),
                    ],
                    axis=1,
                )
                value = jnp.dot(
                    lefts[t, h], jnp.concatenate([both, both], axis=0), preferred_element_type=F32
                )
                value = value[:, :128] + value[:, 128:]
                for k, lanes in ((2 * h, slice(0, BS)), (2 * h + 1, slice(BS, 128))):
                    code = second + at_row(slot, i, k)
                    mask = mask | (1 << code)
                    sums[code, :, lanes] = sums[code, :, lanes] + value[:, lanes]
        return mask

    def flush(p, mask):
        for r in range(2):
            row = owner[jnp.maximum(p * 2 + r, 0)]
            dest = row >> shift
            tag = ((row >> 3) & 7) * 256 + (row & 7)
            start = cnt[dest]
            for s in range(SLOTS):
                c = r * SLOTS + s
                used = (mask >> c) & 1
                meta[dest, 0, start] = tag + s * 4096
                place = jnp.where(used == 1, start, CAP)
                start = start + used
                even = sums[c, pl.ds(0, 32, 2), :]
                odd = sums[c, pl.ds(1, 32, 2), :]
                bucket[dest, place] = jnp.where(low, even, pltpu.roll(odd, BS, 1)) + jnp.where(
                    low, pltpu.roll(even, BS, 1), odd
                )
            cnt[dest] = start

    def own(p):
        return [(blocks, p * 4 + t + 2) for t in range(4)]

    end = NC // 2 - 1

    def step(p, mask, upcoming):
        flush(p - 1, mask)
        mask = second_product(p)
        if upcoming is not None:
            first_product(p + 1, upcoming)
        return mask

    first_product(0, own(0))
    mask = lax.fori_loop(0, end - 1, lambda p, mask: step(p, mask, own(p + 1)), jnp.int32(0))
    mask = step(end - 1, mask, own(end)[:2] + [(nblocks, 0), (nblocks, 1)])
    mask = step(end, mask, None)
    flush(end, mask)

    for d in range(n_gx):
        count = cnt[d]
        meta[d, 0, COUNT] = count
        for u in range(STEP):
            meta[d, 0, count + u] = PANEL


def coarse_buckets(n_gx, n_gy, owner, blocks, nblocks, weights, rows, own_ints, near_ints):
    def kernel(owner, blocks, nblocks, weights, rows, c0, s0, a0, c1, s1, a1, *rest):
        coarse_kernel(
            n_gx, n_gy, owner, blocks, nblocks, weights, rows, (c0, s0, a0), (c1, s1, a1), *rest
        )

    return pl.pallas_call(
        kernel,
        out_shape=(
            jax.ShapeDtypeStruct((n_gx, CAP + 2, 32, 128), F32),
            jax.ShapeDtypeStruct((n_gx, 1, META), jnp.int32),
        ),
        in_specs=[SMEM] + [VMEM] * 4 + [ANY] * 6,
        out_specs=(VMEM, SMEM),
        scratch_shapes=[
            pltpu.SMEM((2, NNZ, 128), jnp.int32),
            pltpu.SMEM((2, NNZ, 128), jnp.int32),
            pltpu.SMEM((2, 1, 128), jnp.int32),
            pltpu.VMEM((4, 2, BS, 256), BF16),
            pltpu.VMEM((2 * SLOTS, BS, 128), F32),
            pltpu.SMEM((n_gx,), jnp.int32),
            pltpu.SemaphoreType.DMA((3, 2)),
        ],
        compiler_params=pltpu.CompilerParams(vmem_limit_bytes=4 << 20),
        name="coarse",
    )(owner, blocks, nblocks, weights, rows, *own_ints, *near_ints)


ORDER = (1, 2, 6, 3, 7, 4, 5)


def flipped(index, k, bits):
    out = 0
    for b in range(bits):
        bit = lax.rem(index // (1 << b), 2)
        out = out + ((1 - bit) if (k >> b) & 1 else bit) * (1 << b)
    return out


def push(src, dst, send, recv, to):
    return pltpu.make_async_remote_copy(
        src_ref=src, dst_ref=dst, send_sem=send, recv_sem=recv, device_id=to, device_id_type=MESH
    )


def greet(others):
    barrier = pltpu.get_barrier_semaphore()
    for other in others:
        pl.semaphore_signal(barrier, inc=1, device_id=other, device_id_type=MESH)
    pl.semaphore_wait(barrier, len(others))


def route_kernel(bucket, meta, got, got_meta, pair, pair_meta, xs, xr, xms, xmr, zs, zr, zms, zmr):
    gx, gy = lax.axis_index("gx"), lax.axis_index("gy")
    n_gx = bucket.shape[0]
    partner = (gx, flipped(gy, 1, 4))
    peer = [None] + [flipped(gx, k, 3) for k in range(1, n_gx)]
    greet([(peer[k], gy) for k in range(1, n_gx)] + [partner])

    def forward(k, src, src_meta):
        made = [
            push(src_meta, pair_meta.at[k], zms.at[k], zmr.at[k], partner),
            push(src, pair.at[k], zs.at[k], zr.at[k], partner),
        ]
        for c in made:
            c.start()
        return made

    onward = forward(0, bucket.at[gx, pl.ds(0, CAP)], meta.at[gx])
    sent = {}
    for k in ORDER:
        to = (peer[k], gy)
        sent[k] = (
            push(meta.at[peer[k]], got_meta.at[k - 1], xms.at[k - 1], xmr.at[k - 1], to),
            push(bucket.at[peer[k], pl.ds(0, CAP)], got.at[k - 1], xs.at[k - 1], xr.at[k - 1], to),
        )
        for c in sent[k]:
            c.start()
    for k in ORDER:
        for c in sent[k]:
            c.wait_recv()
        onward += forward(k, got.at[k - 1], got_meta.at[k - 1])
    for k in ORDER:
        for c in sent[k]:
            c.wait_send()
    for c in onward:
        c.wait()


def route(n_gx, bucket, meta):
    data = lambda n: jax.ShapeDtypeStruct((n, CAP, 32, 128), F32)
    tags = lambda n: jax.ShapeDtypeStruct((n, 1, META), jnp.int32)
    sems = lambda n: pltpu.SemaphoreType.DMA((n,))
    return pl.pallas_call(
        route_kernel,
        out_shape=(data(n_gx - 1), tags(n_gx - 1), data(n_gx), tags(n_gx)),
        in_specs=[ANY] * 2,
        out_specs=[ANY] * 4,
        scratch_shapes=[sems(n_gx - 1)] * 4 + [sems(n_gx)] * 4,
        compiler_params=pltpu.CompilerParams(collective_id=1, has_side_effects=True, vmem_limit_bytes=4 << 20),
        name="route",
    )(bucket, meta)


LEAN = 45
HEAD = 30
TAIL = LEAN - HEAD
EXTRA = 32
VOTES = 7


def lean_kernel(
    bucket, meta, got, got_meta, pair, pair_meta, extra, over,
    tags, spare, ballots, heard, result, xs, xr, xms, xmr, zs, zr, zms, zmr, es, er, vs, vr, ms,
):
    gx, gy = lax.axis_index("gx"), lax.axis_index("gy")
    n_gx = bucket.shape[0]
    partner = (gx, flipped(gy, 1, 4))
    peer = [gx] + [flipped(gx, k, 3) for k in range(1, n_gx)]
    voters = [partner] + [(gx, flipped(gy, k, 4)) for k in (2, 4, 8)] + [(peer[k], gy) for k in (1, 2, 4)]
    greet([(peer[k], gy) for k in range(1, n_gx)] + voters[:4])

    sent_meta = {}
    for k in ORDER:
        sent_meta[k] = push(
            meta.at[peer[k]], got_meta.at[k - 1], xms.at[k - 1], xmr.at[k - 1], (peer[k], gy)
        )
        sent_meta[k].start()
    sent = {}
    for k in ORDER:
        sent[k] = push(
            bucket.at[peer[k], pl.ds(0, LEAN)], got.at[k - 1], xs.at[k - 1], xr.at[k - 1], (peer[k], gy)
        )

    onward = []

    def forward(k, src, src_meta):
        made = [
            push(src_meta, pair_meta.at[k], zms.at[k], zmr.at[k], partner),
            push(src, pair.at[k], zs.at[k], zr.at[k], partner),
        ]
        for c in made:
            c.start()
        onward.extend(made)

    def keep_tags(k, src):
        c = pltpu.make_async_copy(src, tags.at[k], ms.at[k])
        c.start()
        c.wait()

    sent[ORDER[0]].start()
    forward(0, bucket.at[gx, pl.ds(0, HEAD)], meta.at[gx])
    for k in ORDER[1:]:
        sent[k].start()
    keep_tags(0, meta.at[gx])
    for k in ORDER:
        sent_meta[k].wait_recv()
        keep_tags(k, got_meta.at[k - 1])
    counts = [tags[k, 0, COUNT] for k in range(n_gx)]
    beyond = [jnp.maximum(n - HEAD, 0) for n in counts]
    starts = [0]
    for n in beyond:
        starts.append(starts[-1] + n)
    bad = jnp.where(starts[-1] > EXTRA, 1, 0)
    for n in counts:
        bad = jnp.maximum(bad, jnp.where(n > LEAN, 1, 0))
    ballots[0] = jnp.zeros((8, 128), jnp.int32) + bad

    votes = []

    def vote(n):
        c = push(ballots.at[n], heard.at[n], vs.at[n], vr.at[n], voters[n])
        c.start()
        votes.append(c)

    def count(n):
        votes[n].wait_recv()
        ballots[n + 1] = jnp.maximum(ballots[n], heard[n])

    for n, k in enumerate(ORDER):
        sent[k].wait_recv()
        forward(k, got.at[k - 1, pl.ds(0, HEAD)], got_meta.at[k - 1])
        if n > 0:
            count(n - 1)
        vote(n)
    for p in range(EXTRA):
        k, n = 0, p
        for j in range(1, n_gx):
            past = p >= starts[j]
            k = jnp.where(past, j, k)
            n = jnp.where(past, p - starts[j], n)
        at = HEAD + jnp.minimum(n, TAIL - 1)
        spare[p] = jnp.where(k == 0, bucket[gx, at], got[jnp.maximum(k, 1) - 1, at])
    count(VOTES - 1)
    rest = push(spare, extra, es, er, partner)
    rest.start()
    out = pltpu.make_async_copy(ballots.at[VOTES], result, ms.at[0])
    out.start()
    for k in ORDER:
        sent_meta[k].wait_send()
        sent[k].wait_send()
    for c in votes:
        c.wait_send()
    out.wait()
    over[0, 0] = result[0, 0]
    for c in onward:
        c.wait()
    rest.wait()


def lean_route(n_gx, bucket, meta):
    data = lambda n, cap: jax.ShapeDtypeStruct((n, cap, 32, 128), F32)
    tags = lambda n: jax.ShapeDtypeStruct((n, 1, META), jnp.int32)
    sems = lambda *n: pltpu.SemaphoreType.DMA(n)
    return pl.pallas_call(
        lean_kernel,
        out_shape=(
            data(n_gx - 1, LEAN),
            tags(n_gx - 1),
            data(n_gx, HEAD),
            tags(n_gx),
            jax.ShapeDtypeStruct((EXTRA, 32, 128), F32),
            jax.ShapeDtypeStruct((1, 1), jnp.int32),
        ),
        in_specs=[VMEM, ANY],
        out_specs=[VMEM] + [ANY] * 4 + [SMEM],
        scratch_shapes=[
            pltpu.SMEM((n_gx, 1, META), jnp.int32),
            pltpu.VMEM((EXTRA, 32, 128), F32),
            pltpu.VMEM((VOTES + 1, 8, 128), jnp.int32),
            pltpu.VMEM((VOTES, 8, 128), jnp.int32),
            pltpu.SMEM((8, 128), jnp.int32),
        ]
        + [sems(n_gx - 1)] * 4
        + [sems(n_gx)] * 4
        + [sems(), sems(), sems(VOTES), sems(VOTES), sems(n_gx)],
        compiler_params=pltpu.CompilerParams(collective_id=2, has_side_effects=True, vmem_limit_bytes=4 << 20),
        name="lean_route",
    )(bucket, meta)


STEP = 5
PANEL = SLOTS * 16 * 256


def unpack_kernel(n_gx, lean, tags, got_tags, pair_tags, bucket, got, pair, extra, out, *rest):
    panel, osems = rest
    gx, odd = lax.axis_index("gx"), lax.rem(lax.axis_index("gy"), 2)
    own_cap, pair_cap = got.shape[1], pair.shape[1]
    chunks = [(tags, gx, bucket, gx)]
    chunks += [(got_tags, k, got, k) for k in range(n_gx - 1)]
    chunks += [(pair_tags, k, pair, k) for k in range(n_gx)]

    def place(base, tag, block):
        panel[pl.ds(base + tag, 32, 8), :] = block

    stores = []
    for half in range(2):
        base = (odd if half == 0 else 1 - odd) * 2048
        cap = own_cap if half == 0 else pair_cap

        @pl.loop(0, 8)
        def _(g):
            for s in range(SLOTS):
                panel[pl.ds(s * 4096 + base + g * 256, 256), :] = jnp.zeros((256, 128), F32)

        for c in range(n_gx):
            table, k, stage, part = chunks[half * n_gx + c]
            count = jnp.minimum(table[k, 0, COUNT], cap)

            @pl.loop(0, (count + STEP - 1) // STEP)
            def _(b):
                at = [b * STEP + u for u in range(STEP)]
                if not lean:
                    at = [jnp.minimum(n, cap - 1) for n in at]
                found = [stage[part, n] for n in at]
                for u in range(STEP):
                    place(base, table[k, 0, b * STEP + u], found[u])

        if half == 1 and lean:
            at = 0
            for k in range(n_gx):
                beyond = jnp.maximum(pair_tags[k, 0, COUNT] - pair_cap, 0)
                begin = at

                @pl.loop(0, beyond)
                def _(n):
                    place(base, pair_tags[k, 0, pair_cap + n], extra[begin + n])

                at = at + beyond

        for s in range(SLOTS):
            store = pltpu.make_async_copy(
                panel.at[pl.ds(s * 4096 + base, 2048)],
                out.at[pl.ds(s * 4096 + base, 2048)],
                osems.at[half, s],
            )
            store.start()
            stores.append(store)
    for store in stores:
        store.wait()


def unpack(n_gx, lean, tags, got_tags, pair_tags, bucket, got, pair, extra):
    return pl.pallas_call(
        functools.partial(unpack_kernel, n_gx, lean),
        out_shape=jax.ShapeDtypeStruct((PANEL, 128), F32),
        in_specs=[SMEM] * 3 + [VMEM] * 4,
        out_specs=ANY,
        scratch_shapes=[
            pltpu.VMEM((PANEL + 2048 + 256, 128), F32),
            pltpu.SemaphoreType.DMA((2, SLOTS)),
        ],
        compiler_params=pltpu.CompilerParams(vmem_limit_bytes=40 << 20),
        name="unpack_lean" if lean else "unpack_full",
    )(tags, got_tags, pair_tags, bucket, got, pair, extra)


def body(blocks, prolong, columns, aggregate, column_slot, owner_row):
    n_gx, n_gy = lax.axis_size("gx"), lax.axis_size("gy")
    flat = blocks.reshape(NB, NNZ, 32, 128).transpose(0, 2, 1, 3).reshape(NB, 128, 128)
    q = prolong.reshape(16, 8, 32, 128).transpose(0, 2, 1, 3).reshape(16, 256, 128)
    ints = (columns.T, column_slot.T, aggregate.reshape(1, NB))
    nblocks, *near, weights, rows = halo(n_gx, n_gy, flat, q.reshape(16, 32, 8, 128), *ints)
    bucket, meta = coarse_buckets(n_gx, n_gy, owner_row, flat, nblocks, weights, rows, ints, near)
    got, got_meta, pair, pair_meta, extra, over = lean_route(n_gx, bucket, meta)

    def full(_):
        got, got_meta, pair, pair_meta = route(n_gx, bucket, meta)
        return unpack(n_gx, False, meta, got_meta, pair_meta, bucket, got, pair, extra)

    def fitted(_):
        return unpack(n_gx, True, meta, got_meta, pair_meta, bucket, got, pair, extra)

    out = lax.cond(over[0, 0] > 0, full, fitted, 0)
    out = out.reshape(SLOTS, 16, 32, 8, 128).transpose(1, 3, 0, 2, 4)
    return out.reshape(NB, SLOTS, BS * BS)


def solution(mesh):
    placed = (
        P(("gx", "gy"), None, None),
        P(("gx", "gy"), None),
        P(("gx", "gy"), None),
        P(("gx", "gy")),
        P(("gx", "gy"), None),
        P(("gx", "gy")),
    )
    return jax.shard_map(
        body, mesh=mesh, in_specs=placed, out_specs=P(("gx", "gy"), None, None), check_vma=False
    )
```

```python
import functools

import jax
import jax.numpy as jnp
from jax import lax
from jax.experimental import pallas as pl
from jax.experimental.pallas import tpu as pltpu
from jax.sharding import PartitionSpec as P

BS = 64
NNZ = 4
SLOTS = 7
MESH = pl.DeviceIdType.MESH
ANY = pl.BlockSpec(memory_space=pl.ANY)
HBM = pl.BlockSpec(memory_space=pltpu.HBM)
SMEM = pl.BlockSpec(memory_space=pltpu.SMEM)
VMEM = pl.BlockSpec(memory_space=pltpu.VMEM)

ROW_CAP = 9
ROW_BLOCKS = 6
CAP = ROW_CAP * ROW_BLOCKS
META = 128
NB = 128
NC = 64
EXT = NB + 6
F32 = jnp.float32
BF16 = jnp.bfloat16


def split(x):
    hi = x.astype(BF16)
    return hi, (x - hi.astype(F32)).astype(BF16)


def prepare(weights, rows, natural, x, flat):
    low = lax.broadcasted_iota(jnp.int32, (32, 128), 1) < BS
    turned = pltpu.roll(flat, BS, 1)
    zero = jnp.zeros_like(flat)
    natural[0, pl.ds(0, 32, 2), :] = jnp.where(low, flat, zero)
    natural[0, pl.ds(1, 32, 2), :] = jnp.where(low, turned, zero)
    natural[1, pl.ds(0, 32, 2), :] = jnp.where(low, zero, turned)
    natural[1, pl.ds(1, 32, 2), :] = jnp.where(low, zero, flat)
    for side in range(2):
        hi, lo = split(natural[side])
        weights[x, side, 0] = hi
        weights[x, side, 1] = lo
    hi, lo = split(jnp.concatenate([flat[:, :BS], turned[:, :BS]], axis=0))
    rows[x] = jnp.concatenate([hi, lo, hi], axis=0)


def halo_kernel(
    n_gx, n_gy, blocks, prolong, columns, slots, aggregate,
    nblocks, ncolumns, nslots, naggregate, weights, rows, own, nright, nleft, natural, send, recv, sem,
):
    me = lax.axis_index("gx") * n_gy + lax.axis_index("gy")
    total = n_gx * n_gy
    up = lax.rem(me + 1, total)
    down = lax.rem(me + total - 1, total)
    up = (up // n_gy, lax.rem(up, n_gy))
    down = (down // n_gy, lax.rem(down, n_gy))
    fetch = pltpu.make_async_copy(prolong, own, sem)
    fetch.start()
    barrier = pltpu.get_barrier_semaphore()
    for other in (up, down):
        pl.semaphore_signal(barrier, inc=1, device_id=other, device_id_type=MESH)
    pl.semaphore_wait(barrier, 2)
    copies = []
    plan = (
        (columns, ncolumns, down),
        (slots, nslots, down),
        (aggregate, naggregate, down),
        (prolong.at[15, :, pl.ds(7, 1)], nleft, up),
        (prolong.at[0, :, pl.ds(0, 5)], nright, down),
        (blocks.at[pl.ds(0, 2)], nblocks, down),
    )
    for n, (src, dst, to) in enumerate(plan):
        copy = pltpu.make_async_remote_copy(
            src_ref=src,
            dst_ref=dst,
            send_sem=send.at[n],
            recv_sem=recv.at[n],
            device_id=to,
            device_id_type=MESH,
        )
        copy.start()
        copies.append(copy)
    fetch.wait()

    @pl.loop(0, 16)
    def _(g):
        for r in range(8):
            prepare(weights, rows, natural.at[r % 2], g * 8 + r + 1, own[g, :, r, :])

    for copy in copies:
        copy.wait()
    prepare(weights, rows, natural.at[0], 0, nleft[:, 0, :])
    for r in range(5):
        prepare(weights, rows, natural.at[1 - r % 2], NB + 1 + r, nright[:, r, :])


def halo(n_gx, n_gy, blocks, prolong, columns, slots, aggregate):
    return pl.pallas_call(
        functools.partial(halo_kernel, n_gx, n_gy),
        out_shape=(
            jax.ShapeDtypeStruct((2, 128, 128), F32),
            jax.ShapeDtypeStruct((NNZ, 128), jnp.int32),
            jax.ShapeDtypeStruct((NNZ, 128), jnp.int32),
            jax.ShapeDtypeStruct((1, 128), jnp.int32),
            jax.ShapeDtypeStruct((EXT, 2, 2, BS, 128), BF16),
            jax.ShapeDtypeStruct((EXT, 3 * BS, BS), BF16),
        ),
        in_specs=[HBM] * 5,
        out_specs=[ANY] * 4 + [VMEM] * 2,
        scratch_shapes=[
            pltpu.VMEM((16, 32, 8, 128), F32),
            pltpu.VMEM((32, 5, 128), F32),
            pltpu.VMEM((32, 1, 128), F32),
            pltpu.VMEM((2, 2, BS, 128), F32),
            pltpu.SemaphoreType.DMA((6,)),
            pltpu.SemaphoreType.DMA((6,)),
            pltpu.SemaphoreType.DMA(()),
        ],
        compiler_params=pltpu.CompilerParams(collective_id=0, has_side_effects=True, vmem_limit_bytes=4 << 20),
        name="halo",
    )(*(pltpu.with_memory_space_constraint(x, pltpu.HBM) for x in (blocks, prolong, columns, slots, aggregate)))


COUNT = META - 1


def coarse_kernel(
    n_gx, n_gy, owner, blocks, nblocks, weights, rows, own_ints, near_ints, bucket, meta,
    column, slot, parity, lefts, sums, cnt, isems,
):
    first = (lax.axis_index("gx") * n_gy + lax.axis_index("gy")) * NB
    fine = n_gx * n_gy * NB
    shift = (NC * n_gy).bit_length() - 1
    for n, (table, own, near) in enumerate(zip((column, slot, parity), own_ints, near_ints)):
        pltpu.make_async_copy(own, table.at[0], isems.at[n, 0]).start()
        pltpu.make_async_copy(near, table.at[1], isems.at[n, 1]).start()

    for d in range(n_gx):
        cnt[d] = 0
    low = lax.broadcasted_iota(jnp.int32, (32, 128), 1) < BS

    for n, (table, own, near) in enumerate(zip((column, slot, parity), own_ints, near_ints)):
        pltpu.make_async_copy(own, table.at[0], isems.at[n, 0]).wait()
        pltpu.make_async_copy(near, table.at[1], isems.at[n, 1]).wait()

    def at_row(table, i, k):
        return table[i >> 7, k, i & 127]

    def first_product(p, block_rows):
        for t in range(4):
            i = p * 4 + t + 2
            source, at = block_rows[t]
            parts = [source[at, pl.ds(k, 32, 4), :] for k in range(NNZ)]
            turned = [pltpu.roll(part, BS, 1) for part in parts]
            top = [jnp.where(low, parts[k], turned[k + 1]) for k in (0, 2)]
            bottom = [jnp.where(low, turned[k], parts[k + 1]) for k in (0, 2)]
            hi, lo = split(
                jnp.concatenate([jnp.concatenate(top, axis=1), jnp.concatenate(bottom, axis=1)], axis=0)
            )
            left = lax.dot_general(
                rows[i + 1],
                jnp.concatenate([hi, hi, lo], axis=0),
                (((0,), (0,)), ((), ())),
                preferred_element_type=F32,
            )
            hi, lo = split(left)
            for h in range(2):
                lanes = slice(h * 128, h * 128 + 128)
                lefts[t, h, :, :128] = hi[:, lanes]
                lefts[t, h, :, 128:] = lo[:, lanes]

    def second_product(p):
        sums[...] = jnp.zeros_like(sums)
        mask = 0
        for t in range(4):
            i = p * 4 + t + 2
            second = (at_row(parity, i, 0) & 1) * SLOTS
            for h in range(2):
                a, b = [
                    (at_row(column, i, k) - first + 1) & (fine - 1) for k in (2 * h, 2 * h + 1)
                ]
                both = jnp.concatenate(
                    [
                        jnp.concatenate([weights[a, 0, 0], weights[b, 1, 0]], axis=0),
                        jnp.concatenate([weights[a, 0, 1], weights[b, 1, 1]], axis=0),
                    ],
                    axis=1,
                )
                value = jnp.dot(
                    lefts[t, h], jnp.concatenate([both, both], axis=0), preferred_element_type=F32
                )
                value = value[:, :128] + value[:, 128:]
                for k, lanes in ((2 * h, slice(0, BS)), (2 * h + 1, slice(BS, 128))):
                    code = second + at_row(slot, i, k)
                    mask = mask | (1 << code)
                    sums[code, :, lanes] = sums[code, :, lanes] + value[:, lanes]
        return mask

    def flush(p, mask):
        for r in range(2):
            row = owner[jnp.maximum(p * 2 + r, 0)]
            dest = row >> shift
            tag = ((row >> 3) & 7) * 256 + (row & 7)
            start = cnt[dest]
            for s in range(SLOTS):
                c = r * SLOTS + s
                used = (mask >> c) & 1
                meta[dest, 0, start] = tag + s * 4096
                place = jnp.where(used == 1, start, CAP)
                start = start + used
                even = sums[c, pl.ds(0, 32, 2), :]
                odd = sums[c, pl.ds(1, 32, 2), :]
                bucket[dest, place] = jnp.where(low, even, pltpu.roll(odd, BS, 1)) + jnp.where(
                    low, pltpu.roll(even, BS, 1), odd
                )
            cnt[dest] = start

    def own(p):
        return [(blocks, p * 4 + t + 2) for t in range(4)]

    end = NC // 2 - 1

    def step(p, mask, upcoming):
        flush(p - 1, mask)
        mask = second_product(p)
        if upcoming is not None:
            first_product(p + 1, upcoming)
        return mask

    first_product(0, own(0))
    mask = lax.fori_loop(0, end - 1, lambda p, mask: step(p, mask, own(p + 1)), jnp.int32(0))
    mask = step(end - 1, mask, own(end)[:2] + [(nblocks, 0), (nblocks, 1)])
    mask = step(end, mask, None)
    flush(end, mask)

    for d in range(n_gx):
        count = cnt[d]
        meta[d, 0, COUNT] = count
        for u in range(STEP):
            meta[d, 0, count + u] = PANEL


def coarse_buckets(n_gx, n_gy, owner, blocks, nblocks, weights, rows, own_ints, near_ints):
    def kernel(owner, blocks, nblocks, weights, rows, c0, s0, a0, c1, s1, a1, *rest):
        coarse_kernel(
            n_gx, n_gy, owner, blocks, nblocks, weights, rows, (c0, s0, a0), (c1, s1, a1), *rest
        )

    return pl.pallas_call(
        kernel,
        out_shape=(
            jax.ShapeDtypeStruct((n_gx, CAP + 2, 32, 128), F32),
            jax.ShapeDtypeStruct((n_gx, 1, META), jnp.int32),
        ),
        in_specs=[SMEM] + [VMEM] * 4 + [ANY] * 6,
        out_specs=(VMEM, SMEM),
        scratch_shapes=[
            pltpu.SMEM((2, NNZ, 128), jnp.int32),
            pltpu.SMEM((2, NNZ, 128), jnp.int32),
            pltpu.SMEM((2, 1, 128), jnp.int32),
            pltpu.VMEM((4, 2, BS, 256), BF16),
            pltpu.VMEM((2 * SLOTS, BS, 128), F32),
            pltpu.SMEM((n_gx,), jnp.int32),
            pltpu.SemaphoreType.DMA((3, 2)),
        ],
        compiler_params=pltpu.CompilerParams(vmem_limit_bytes=4 << 20),
        name="coarse",
    )(owner, blocks, nblocks, weights, rows, *own_ints, *near_ints)


ORDER = (1, 2, 6, 3, 7, 4, 5)


def flipped(index, k, bits):
    out = 0
    for b in range(bits):
        bit = lax.rem(index // (1 << b), 2)
        out = out + ((1 - bit) if (k >> b) & 1 else bit) * (1 << b)
    return out


def push(src, dst, send, recv, to):
    return pltpu.make_async_remote_copy(
        src_ref=src, dst_ref=dst, send_sem=send, recv_sem=recv, device_id=to, device_id_type=MESH
    )


def greet(others):
    barrier = pltpu.get_barrier_semaphore()
    for other in others:
        pl.semaphore_signal(barrier, inc=1, device_id=other, device_id_type=MESH)
    pl.semaphore_wait(barrier, len(others))


def route_kernel(bucket, meta, got, got_meta, pair, pair_meta, xs, xr, xms, xmr, zs, zr, zms, zmr):
    gx, gy = lax.axis_index("gx"), lax.axis_index("gy")
    n_gx = bucket.shape[0]
    partner = (gx, flipped(gy, 1, 4))
    peer = [None] + [flipped(gx, k, 3) for k in range(1, n_gx)]
    greet([(peer[k], gy) for k in range(1, n_gx)] + [partner])

    def forward(k, src, src_meta):
        made = [
            push(src_meta, pair_meta.at[k], zms.at[k], zmr.at[k], partner),
            push(src, pair.at[k], zs.at[k], zr.at[k], partner),
        ]
        for c in made:
            c.start()
        return made

    onward = forward(0, bucket.at[gx, pl.ds(0, CAP)], meta.at[gx])
    sent = {}
    for k in ORDER:
        to = (peer[k], gy)
        sent[k] = (
            push(meta.at[peer[k]], got_meta.at[k - 1], xms.at[k - 1], xmr.at[k - 1], to),
            push(bucket.at[peer[k], pl.ds(0, CAP)], got.at[k - 1], xs.at[k - 1], xr.at[k - 1], to),
        )
        for c in sent[k]:
            c.start()
    for k in ORDER:
        for c in sent[k]:
            c.wait_recv()
        onward += forward(k, got.at[k - 1], got_meta.at[k - 1])
    for k in ORDER:
        for c in sent[k]:
            c.wait_send()
    for c in onward:
        c.wait()


def route(n_gx, bucket, meta):
    data = lambda n: jax.ShapeDtypeStruct((n, CAP, 32, 128), F32)
    tags = lambda n: jax.ShapeDtypeStruct((n, 1, META), jnp.int32)
    sems = lambda n: pltpu.SemaphoreType.DMA((n,))
    return pl.pallas_call(
        route_kernel,
        out_shape=(data(n_gx - 1), tags(n_gx - 1), data(n_gx), tags(n_gx)),
        in_specs=[ANY] * 2,
        out_specs=[ANY] * 4,
        scratch_shapes=[sems(n_gx - 1)] * 4 + [sems(n_gx)] * 4,
        compiler_params=pltpu.CompilerParams(collective_id=1, has_side_effects=True, vmem_limit_bytes=4 << 20),
        name="route",
    )(bucket, meta)


LEAN = 45
HEAD = 30
TAIL = LEAN - HEAD
EXTRA = 32
VOTES = 7
VIA = {4: (2, 6), 5: (6, 3)}
AFTER = 4


def lean_kernel(
    bucket, meta, got, got_meta, pair, pair_meta, extra, over,
    tags, spare, relay, ballots, heard, result, hs, hr, xs, xr, xms, xmr, zs, zr, zms, zmr, es, er, vs, vr, ms,
):
    gx, gy = lax.axis_index("gx"), lax.axis_index("gy")
    n_gx = bucket.shape[0]
    partner = (gx, flipped(gy, 1, 4))
    peer = [gx] + [flipped(gx, k, 3) for k in range(1, n_gx)]
    voters = [partner] + [(gx, flipped(gy, k, 4)) for k in (2, 4, 8)] + [(peer[k], gy) for k in (1, 2, 4)]
    greet([(peer[k], gy) for k in range(1, n_gx)] + voters[:4])

    sent_meta = {}
    for k in ORDER:
        sent_meta[k] = push(
            meta.at[peer[k]], got_meta.at[k - 1], xms.at[k - 1], xmr.at[k - 1], (peer[k], gy)
        )
        sent_meta[k].start()
    sent = {}
    for k in ORDER:
        if k not in VIA:
            sent[k] = push(
                bucket.at[peer[k], pl.ds(0, LEAN)], got.at[k - 1], xs.at[k - 1], xr.at[k - 1], (peer[k], gy)
            )
    hops = {}
    for n, (k, (first, second)) in enumerate(VIA.items()):
        hops[k] = push(bucket.at[peer[k], pl.ds(0, LEAN)], relay.at[n], hs.at[n], hr.at[n], (peer[first], gy))
        sent[k] = push(relay.at[n], got.at[k - 1], xs.at[k - 1], xr.at[k - 1], (peer[second], gy))

    onward = []

    def forward(k, src, src_meta):
        made = [
            push(src_meta, pair_meta.at[k], zms.at[k], zmr.at[k], partner),
            push(src, pair.at[k], zs.at[k], zr.at[k], partner),
        ]
        for c in made:
            c.start()
        onward.extend(made)

    def keep_tags(k, src):
        c = pltpu.make_async_copy(src, tags.at[k], ms.at[k])
        c.start()
        c.wait()

    sent[ORDER[0]].start()
    forward(0, bucket.at[gx, pl.ds(0, HEAD)], meta.at[gx])
    for k in ORDER[1:]:
        hops.get(k, sent[k]).start()
    keep_tags(0, meta.at[gx])
    for k in ORDER:
        sent_meta[k].wait_recv()
        keep_tags(k, got_meta.at[k - 1])
    counts = [tags[k, 0, COUNT] for k in range(n_gx)]
    beyond = [jnp.maximum(n - HEAD, 0) for n in counts]
    starts = [0]
    for n in beyond:
        starts.append(starts[-1] + n)
    bad = jnp.where(starts[-1] > EXTRA, 1, 0)
    for n in counts:
        bad = jnp.maximum(bad, jnp.where(n > LEAN, 1, 0))
    ballots[0] = jnp.zeros((8, 128), jnp.int32) + bad

    votes = []

    def vote(n):
        c = push(ballots.at[n], heard.at[n], vs.at[n], vr.at[n], voters[n])
        c.start()
        votes.append(c)

    def count(n):
        votes[n].wait_recv()
        ballots[n + 1] = jnp.maximum(ballots[n], heard[n])

    for n, k in enumerate(ORDER):
        if k == AFTER:
            for j in VIA:
                hops[j].wait_recv()
                sent[j].start()
        sent[k].wait_recv()
        forward(k, got.at[k - 1, pl.ds(0, HEAD)], got_meta.at[k - 1])
        if n == 3:
            count(0)
        if n == 5:
            count(1)
        if n in (1, 3):
            vote(n // 2)
    for p in range(EXTRA):
        k, n = 0, p
        for j in range(1, n_gx):
            past = p >= starts[j]
            k = jnp.where(past, j, k)
            n = jnp.where(past, p - starts[j], n)
        at = HEAD + jnp.minimum(n, TAIL - 1)
        spare[p] = jnp.where(k == 0, bucket[gx, at], got[jnp.maximum(k, 1) - 1, at])
    rest = push(spare, extra, es, er, partner)
    rest.start()
    for n in range(2, VOTES):
        vote(n)
        count(n)
    out = pltpu.make_async_copy(ballots.at[VOTES], result, ms.at[0])
    out.start()
    for k in ORDER:
        sent_meta[k].wait_send()
        sent[k].wait_send()
    for k in VIA:
        hops[k].wait_send()
    for c in votes:
        c.wait_send()
    out.wait()
    over[0, 0] = result[0, 0]
    for c in onward:
        c.wait()
    rest.wait()


def lean_route(n_gx, bucket, meta):
    data = lambda n, cap: jax.ShapeDtypeStruct((n, cap, 32, 128), F32)
    tags = lambda n: jax.ShapeDtypeStruct((n, 1, META), jnp.int32)
    sems = lambda *n: pltpu.SemaphoreType.DMA(n)
    return pl.pallas_call(
        lean_kernel,
        out_shape=(
            data(n_gx - 1, LEAN),
            tags(n_gx - 1),
            data(n_gx, HEAD),
            tags(n_gx),
            jax.ShapeDtypeStruct((EXTRA, 32, 128), F32),
            jax.ShapeDtypeStruct((1, 1), jnp.int32),
        ),
        in_specs=[VMEM, ANY],
        out_specs=[VMEM] + [ANY] * 4 + [SMEM],
        scratch_shapes=[
            pltpu.SMEM((n_gx, 1, META), jnp.int32),
            pltpu.VMEM((EXTRA, 32, 128), F32),
            pltpu.VMEM((len(VIA), LEAN, 32, 128), F32),
            pltpu.VMEM((VOTES + 1, 8, 128), jnp.int32),
            pltpu.VMEM((VOTES, 8, 128), jnp.int32),
            pltpu.SMEM((8, 128), jnp.int32),
        ]
        + [sems(len(VIA))] * 2
        + [sems(n_gx - 1)] * 4
        + [sems(n_gx)] * 4
        + [sems(), sems(), sems(VOTES), sems(VOTES), sems(n_gx)],
        compiler_params=pltpu.CompilerParams(collective_id=2, has_side_effects=True, vmem_limit_bytes=4 << 20),
        name="lean_route",
    )(bucket, meta)


STEP = 5
PANEL = SLOTS * 16 * 256


def unpack_kernel(n_gx, lean, tags, got_tags, pair_tags, bucket, got, pair, extra, out, *rest):
    panel, osems = rest
    gx, odd = lax.axis_index("gx"), lax.rem(lax.axis_index("gy"), 2)
    own_cap, pair_cap = got.shape[1], pair.shape[1]
    chunks = [(tags, gx, bucket, gx)]
    chunks += [(got_tags, k, got, k) for k in range(n_gx - 1)]
    chunks += [(pair_tags, k, pair, k) for k in range(n_gx)]

    def place(base, tag, block):
        panel[pl.ds(base + tag, 32, 8), :] = block

    stores = []
    for half in range(2):
        base = (odd if half == 0 else 1 - odd) * 2048
        cap = own_cap if half == 0 else pair_cap

        @pl.loop(0, 8)
        def _(g):
            for s in range(SLOTS):
                panel[pl.ds(s * 4096 + base + g * 256, 256), :] = jnp.zeros((256, 128), F32)

        for c in range(n_gx):
            table, k, stage, part = chunks[half * n_gx + c]
            count = jnp.minimum(table[k, 0, COUNT], cap)

            @pl.loop(0, (count + STEP - 1) // STEP)
            def _(b):
                at = [b * STEP + u for u in range(STEP)]
                if not lean:
                    at = [jnp.minimum(n, cap - 1) for n in at]
                found = [stage[part, n] for n in at]
                for u in range(STEP):
                    place(base, table[k, 0, b * STEP + u], found[u])

        if half == 1 and lean:
            at = 0
            for k in range(n_gx):
                beyond = jnp.maximum(pair_tags[k, 0, COUNT] - pair_cap, 0)
                begin = at

                @pl.loop(0, beyond)
                def _(n):
                    place(base, pair_tags[k, 0, pair_cap + n], extra[begin + n])

                at = at + beyond

        for s in range(SLOTS):
            store = pltpu.make_async_copy(
                panel.at[pl.ds(s * 4096 + base, 2048)],
                out.at[pl.ds(s * 4096 + base, 2048)],
                osems.at[half, s],
            )
            store.start()
            stores.append(store)
    for store in stores:
        store.wait()


def unpack(n_gx, lean, tags, got_tags, pair_tags, bucket, got, pair, extra):
    return pl.pallas_call(
        functools.partial(unpack_kernel, n_gx, lean),
        out_shape=jax.ShapeDtypeStruct((PANEL, 128), F32),
        in_specs=[SMEM] * 3 + [VMEM] * 4,
        out_specs=ANY,
        scratch_shapes=[
            pltpu.VMEM((PANEL + 2048 + 256, 128), F32),
            pltpu.SemaphoreType.DMA((2, SLOTS)),
        ],
        compiler_params=pltpu.CompilerParams(vmem_limit_bytes=40 << 20),
        name="unpack_lean" if lean else "unpack_full",
    )(tags, got_tags, pair_tags, bucket, got, pair, extra)


def body(blocks, prolong, columns, aggregate, column_slot, owner_row):
    n_gx, n_gy = lax.axis_size("gx"), lax.axis_size("gy")
    flat = blocks.reshape(NB, NNZ, 32, 128).transpose(0, 2, 1, 3).reshape(NB, 128, 128)
    q = prolong.reshape(16, 8, 32, 128).transpose(0, 2, 1, 3).reshape(16, 256, 128)
    ints = (columns.T, column_slot.T, aggregate.reshape(1, NB))
    nblocks, *near, weights, rows = halo(n_gx, n_gy, flat, q.reshape(16, 32, 8, 128), *ints)
    bucket, meta = coarse_buckets(n_gx, n_gy, owner_row, flat, nblocks, weights, rows, ints, near)
    got, got_meta, pair, pair_meta, extra, over = lean_route(n_gx, bucket, meta)

    def full(_):
        got, got_meta, pair, pair_meta = route(n_gx, bucket, meta)
        return unpack(n_gx, False, meta, got_meta, pair_meta, bucket, got, pair, extra)

    def fitted(_):
        return unpack(n_gx, True, meta, got_meta, pair_meta, bucket, got, pair, extra)

    out = lax.cond(over[0, 0] > 0, full, fitted, 0)
    out = out.reshape(SLOTS, 16, 32, 8, 128).transpose(1, 3, 0, 2, 4)
    return out.reshape(NB, SLOTS, BS * BS)


def solution(mesh):
    placed = (
        P(("gx", "gy"), None, None),
        P(("gx", "gy"), None),
        P(("gx", "gy"), None),
        P(("gx", "gy")),
        P(("gx", "gy"), None),
        P(("gx", "gy")),
    )
    return jax.shard_map(
        body, mesh=mesh, in_specs=placed, out_specs=P(("gx", "gy"), None, None), check_vma=False
    )
```

```python
import functools

import jax
import jax.numpy as jnp
from jax import lax
from jax.experimental import pallas as pl
from jax.experimental.pallas import tpu as pltpu
from jax.sharding import PartitionSpec as P

BS = 64
NNZ = 4
SLOTS = 7
MESH = pl.DeviceIdType.MESH
ANY = pl.BlockSpec(memory_space=pl.ANY)
HBM = pl.BlockSpec(memory_space=pltpu.HBM)
SMEM = pl.BlockSpec(memory_space=pltpu.SMEM)
VMEM = pl.BlockSpec(memory_space=pltpu.VMEM)

ROW_CAP = 9
ROW_BLOCKS = 6
CAP = ROW_CAP * ROW_BLOCKS
META = 128
NB = 128
NC = 64
EXT = NB + 6
F32 = jnp.float32
BF16 = jnp.bfloat16


def split(x):
    hi = x.astype(BF16)
    return hi, (x - hi.astype(F32)).astype(BF16)


def prepare(weights, rows, natural, x, flat):
    low = lax.broadcasted_iota(jnp.int32, (32, 128), 1) < BS
    turned = pltpu.roll(flat, BS, 1)
    zero = jnp.zeros_like(flat)
    natural[0, pl.ds(0, 32, 2), :] = jnp.where(low, flat, zero)
    natural[0, pl.ds(1, 32, 2), :] = jnp.where(low, turned, zero)
    natural[1, pl.ds(0, 32, 2), :] = jnp.where(low, zero, turned)
    natural[1, pl.ds(1, 32, 2), :] = jnp.where(low, zero, flat)
    for side in range(2):
        hi, lo = split(natural[side])
        weights[x, side, 0] = hi
        weights[x, side, 1] = lo
    hi, lo = split(jnp.concatenate([flat[:, :BS], turned[:, :BS]], axis=0))
    rows[x] = jnp.concatenate([hi, lo, hi], axis=0)


def halo_kernel(
    n_gx, n_gy, blocks, prolong, columns, slots, aggregate,
    nblocks, ncolumns, nslots, naggregate, weights, rows, own, nright, nleft, natural, send, recv, sem,
):
    me = lax.axis_index("gx") * n_gy + lax.axis_index("gy")
    total = n_gx * n_gy
    up = lax.rem(me + 1, total)
    down = lax.rem(me + total - 1, total)
    up = (up // n_gy, lax.rem(up, n_gy))
    down = (down // n_gy, lax.rem(down, n_gy))
    fetch = pltpu.make_async_copy(prolong, own, sem)
    fetch.start()
    barrier = pltpu.get_barrier_semaphore()
    for other in (up, down):
        pl.semaphore_signal(barrier, inc=1, device_id=other, device_id_type=MESH)
    pl.semaphore_wait(barrier, 2)
    copies = []
    plan = (
        (columns, ncolumns, down),
        (slots, nslots, down),
        (aggregate, naggregate, down),
        (prolong.at[15, :, pl.ds(7, 1)], nleft, up),
        (prolong.at[0, :, pl.ds(0, 5)], nright, down),
        (blocks.at[pl.ds(0, 2)], nblocks, down),
    )
    for n, (src, dst, to) in enumerate(plan):
        copy = pltpu.make_async_remote_copy(
            src_ref=src,
            dst_ref=dst,
            send_sem=send.at[n],
            recv_sem=recv.at[n],
            device_id=to,
            device_id_type=MESH,
        )
        copy.start()
        copies.append(copy)
    fetch.wait()

    @pl.loop(0, 16)
    def _(g):
        for r in range(8):
            prepare(weights, rows, natural.at[r % 2], g * 8 + r + 1, own[g, :, r, :])

    for copy in copies:
        copy.wait()
    prepare(weights, rows, natural.at[0], 0, nleft[:, 0, :])
    for r in range(5):
        prepare(weights, rows, natural.at[1 - r % 2], NB + 1 + r, nright[:, r, :])


def halo(n_gx, n_gy, blocks, prolong, columns, slots, aggregate):
    return pl.pallas_call(
        functools.partial(halo_kernel, n_gx, n_gy),
        out_shape=(
            jax.ShapeDtypeStruct((2, 128, 128), F32),
            jax.ShapeDtypeStruct((NNZ, 128), jnp.int32),
            jax.ShapeDtypeStruct((NNZ, 128), jnp.int32),
            jax.ShapeDtypeStruct((1, 128), jnp.int32),
            jax.ShapeDtypeStruct((EXT, 2, 2, BS, 128), BF16),
            jax.ShapeDtypeStruct((EXT, 3 * BS, BS), BF16),
        ),
        in_specs=[HBM] * 5,
        out_specs=[ANY] * 4 + [VMEM] * 2,
        scratch_shapes=[
            pltpu.VMEM((16, 32, 8, 128), F32),
            pltpu.VMEM((32, 5, 128), F32),
            pltpu.VMEM((32, 1, 128), F32),
            pltpu.VMEM((2, 2, BS, 128), F32),
            pltpu.SemaphoreType.DMA((6,)),
            pltpu.SemaphoreType.DMA((6,)),
            pltpu.SemaphoreType.DMA(()),
        ],
        compiler_params=pltpu.CompilerParams(collective_id=0, has_side_effects=True, vmem_limit_bytes=4 << 20),
        name="halo",
    )(*(pltpu.with_memory_space_constraint(x, pltpu.HBM) for x in (blocks, prolong, columns, slots, aggregate)))


COUNT = META - 1


def coarse_kernel(
    n_gx, n_gy, owner, blocks, nblocks, weights, rows, own_ints, near_ints, bucket, meta,
    column, slot, parity, lefts, sums, cnt, isems,
):
    first = (lax.axis_index("gx") * n_gy + lax.axis_index("gy")) * NB
    fine = n_gx * n_gy * NB
    shift = (NC * n_gy).bit_length() - 1
    for n, (table, own, near) in enumerate(zip((column, slot, parity), own_ints, near_ints)):
        pltpu.make_async_copy(own, table.at[0], isems.at[n, 0]).start()
        pltpu.make_async_copy(near, table.at[1], isems.at[n, 1]).start()

    for d in range(n_gx):
        cnt[d] = 0
    low = lax.broadcasted_iota(jnp.int32, (32, 128), 1) < BS

    for n, (table, own, near) in enumerate(zip((column, slot, parity), own_ints, near_ints)):
        pltpu.make_async_copy(own, table.at[0], isems.at[n, 0]).wait()
        pltpu.make_async_copy(near, table.at[1], isems.at[n, 1]).wait()

    def at_row(table, i, k):
        return table[i >> 7, k, i & 127]

    def first_product(p, block_rows):
        for t in range(4):
            i = p * 4 + t + 2
            source, at = block_rows[t]
            parts = [source[at, pl.ds(k, 32, 4), :] for k in range(NNZ)]
            turned = [pltpu.roll(part, BS, 1) for part in parts]
            top = [jnp.where(low, parts[k], turned[k + 1]) for k in (0, 2)]
            bottom = [jnp.where(low, turned[k], parts[k + 1]) for k in (0, 2)]
            hi, lo = split(
                jnp.concatenate([jnp.concatenate(top, axis=1), jnp.concatenate(bottom, axis=1)], axis=0)
            )
            left = lax.dot_general(
                rows[i + 1],
                jnp.concatenate([hi, hi, lo], axis=0),
                (((0,), (0,)), ((), ())),
                preferred_element_type=F32,
            )
            hi, lo = split(left)
            for h in range(2):
                lanes = slice(h * 128, h * 128 + 128)
                lefts[t, h, :, :128] = hi[:, lanes]
                lefts[t, h, :, 128:] = lo[:, lanes]

    def second_product(p):
        sums[...] = jnp.zeros_like(sums)
        mask = 0
        for t in range(4):
            i = p * 4 + t + 2
            second = (at_row(parity, i, 0) & 1) * SLOTS
            for h in range(2):
                a, b = [
                    (at_row(column, i, k) - first + 1) & (fine - 1) for k in (2 * h, 2 * h + 1)
                ]
                both = jnp.concatenate(
                    [
                        jnp.concatenate([weights[a, 0, 0], weights[b, 1, 0]], axis=0),
                        jnp.concatenate([weights[a, 0, 1], weights[b, 1, 1]], axis=0),
                    ],
                    axis=1,
                )
                value = jnp.dot(
                    lefts[t, h], jnp.concatenate([both, both], axis=0), preferred_element_type=F32
                )
                value = value[:, :128] + value[:, 128:]
                for k, lanes in ((2 * h, slice(0, BS)), (2 * h + 1, slice(BS, 128))):
                    code = second + at_row(slot, i, k)
                    mask = mask | (1 << code)
                    sums[code, :, lanes] = sums[code, :, lanes] + value[:, lanes]
        return mask

    def flush(p, mask):
        for r in range(2):
            row = owner[jnp.maximum(p * 2 + r, 0)]
            dest = row >> shift
            tag = ((row >> 3) & 7) * 256 + (row & 7)
            start = cnt[dest]
            for s in range(SLOTS):
                c = r * SLOTS + s
                used = (mask >> c) & 1
                meta[dest, 0, start] = tag + s * 4096
                place = jnp.where(used == 1, start, CAP)
                start = start + used
                even = sums[c, pl.ds(0, 32, 2), :]
                odd = sums[c, pl.ds(1, 32, 2), :]
                bucket[dest, place] = jnp.where(low, even, pltpu.roll(odd, BS, 1)) + jnp.where(
                    low, pltpu.roll(even, BS, 1), odd
                )
            cnt[dest] = start

    def own(p):
        return [(blocks, p * 4 + t + 2) for t in range(4)]

    end = NC // 2 - 1

    def step(p, mask, upcoming):
        flush(p - 1, mask)
        mask = second_product(p)
        if upcoming is not None:
            first_product(p + 1, upcoming)
        return mask

    first_product(0, own(0))
    mask = lax.fori_loop(0, end - 1, lambda p, mask: step(p, mask, own(p + 1)), jnp.int32(0))
    mask = step(end - 1, mask, own(end)[:2] + [(nblocks, 0), (nblocks, 1)])
    mask = step(end, mask, None)
    flush(end, mask)

    for d in range(n_gx):
        count = cnt[d]
        meta[d, 0, COUNT] = count
        for u in range(STEP):
            meta[d, 0, count + u] = PANEL


def coarse_buckets(n_gx, n_gy, owner, blocks, nblocks, weights, rows, own_ints, near_ints):
    def kernel(owner, blocks, nblocks, weights, rows, c0, s0, a0, c1, s1, a1, *rest):
        coarse_kernel(
            n_gx, n_gy, owner, blocks, nblocks, weights, rows, (c0, s0, a0), (c1, s1, a1), *rest
        )

    return pl.pallas_call(
        kernel,
        out_shape=(
            jax.ShapeDtypeStruct((n_gx, CAP + 2, 32, 128), F32),
            jax.ShapeDtypeStruct((n_gx, 1, META), jnp.int32),
        ),
        in_specs=[SMEM] + [VMEM] * 4 + [ANY] * 6,
        out_specs=(VMEM, SMEM),
        scratch_shapes=[
            pltpu.SMEM((2, NNZ, 128), jnp.int32),
            pltpu.SMEM((2, NNZ, 128), jnp.int32),
            pltpu.SMEM((2, 1, 128), jnp.int32),
            pltpu.VMEM((4, 2, BS, 256), BF16),
            pltpu.VMEM((2 * SLOTS, BS, 128), F32),
            pltpu.SMEM((n_gx,), jnp.int32),
            pltpu.SemaphoreType.DMA((3, 2)),
        ],
        compiler_params=pltpu.CompilerParams(vmem_limit_bytes=4 << 20),
        name="coarse",
    )(owner, blocks, nblocks, weights, rows, *own_ints, *near_ints)


ORDER = (1, 2, 6, 3, 7, 4, 5)


def flipped(index, k, bits):
    out = 0
    for b in range(bits):
        bit = lax.rem(index // (1 << b), 2)
        out = out + ((1 - bit) if (k >> b) & 1 else bit) * (1 << b)
    return out


def push(src, dst, send, recv, to):
    return pltpu.make_async_remote_copy(
        src_ref=src, dst_ref=dst, send_sem=send, recv_sem=recv, device_id=to, device_id_type=MESH
    )


def greet(others):
    barrier = pltpu.get_barrier_semaphore()
    for other in others:
        pl.semaphore_signal(barrier, inc=1, device_id=other, device_id_type=MESH)
    pl.semaphore_wait(barrier, len(others))


def route_kernel(bucket, meta, got, got_meta, pair, pair_meta, xs, xr, xms, xmr, zs, zr, zms, zmr):
    gx, gy = lax.axis_index("gx"), lax.axis_index("gy")
    n_gx = bucket.shape[0]
    partner = (gx, flipped(gy, 1, 4))
    peer = [None] + [flipped(gx, k, 3) for k in range(1, n_gx)]
    greet([(peer[k], gy) for k in range(1, n_gx)] + [partner])

    def forward(k, src, src_meta):
        made = [
            push(src_meta, pair_meta.at[k], zms.at[k], zmr.at[k], partner),
            push(src, pair.at[k], zs.at[k], zr.at[k], partner),
        ]
        for c in made:
            c.start()
        return made

    onward = forward(0, bucket.at[gx, pl.ds(0, CAP)], meta.at[gx])
    sent = {}
    for k in ORDER:
        to = (peer[k], gy)
        sent[k] = (
            push(meta.at[peer[k]], got_meta.at[k - 1], xms.at[k - 1], xmr.at[k - 1], to),
            push(bucket.at[peer[k], pl.ds(0, CAP)], got.at[k - 1], xs.at[k - 1], xr.at[k - 1], to),
        )
        for c in sent[k]:
            c.start()
    for k in ORDER:
        for c in sent[k]:
            c.wait_recv()
        onward += forward(k, got.at[k - 1], got_meta.at[k - 1])
    for k in ORDER:
        for c in sent[k]:
            c.wait_send()
    for c in onward:
        c.wait()


def route(n_gx, bucket, meta):
    data = lambda n: jax.ShapeDtypeStruct((n, CAP, 32, 128), F32)
    tags = lambda n: jax.ShapeDtypeStruct((n, 1, META), jnp.int32)
    sems = lambda n: pltpu.SemaphoreType.DMA((n,))
    return pl.pallas_call(
        route_kernel,
        out_shape=(data(n_gx - 1), tags(n_gx - 1), data(n_gx), tags(n_gx)),
        in_specs=[ANY] * 2,
        out_specs=[ANY] * 4,
        scratch_shapes=[sems(n_gx - 1)] * 4 + [sems(n_gx)] * 4,
        compiler_params=pltpu.CompilerParams(collective_id=1, has_side_effects=True, vmem_limit_bytes=4 << 20),
        name="route",
    )(bucket, meta)


LEAN = 45
HEAD = 30
TAIL = LEAN - HEAD
EXTRA = 32
VOTES = 7
VIA = {4: (2, 6), 5: (6, 3)}
AFTER = 4


def lean_kernel(
    bucket, meta, got, got_meta, pair, pair_meta, extra, over,
    tags, spare, relay, ballots, heard, result, hs, hr, ts, tr, xs, xr, xms, xmr, zs, zr, zms, zmr, es, er, vs, vr, ms,
):
    gx, gy = lax.axis_index("gx"), lax.axis_index("gy")
    n_gx = bucket.shape[0]
    partner = (gx, flipped(gy, 1, 4))
    peer = [gx] + [flipped(gx, k, 3) for k in range(1, n_gx)]
    voters = [partner] + [(gx, flipped(gy, k, 4)) for k in (2, 4, 8)] + [(peer[k], gy) for k in (1, 2, 4)]
    greet([(peer[k], gy) for k in range(1, n_gx)] + voters[:4])

    sent_meta = {}
    for k in ORDER:
        sent_meta[k] = push(
            meta.at[peer[k]], got_meta.at[k - 1], xms.at[k - 1], xmr.at[k - 1], (peer[k], gy)
        )
        sent_meta[k].start()
    head, tail = pl.ds(0, HEAD), pl.ds(HEAD, TAIL)
    sent = {}
    for k in ORDER:
        if k not in VIA:
            sent[k] = push(
                bucket.at[peer[k], head], got.at[k - 1, head], xs.at[k - 1], xr.at[k - 1], (peer[k], gy)
            )
    hops = {}
    ends = {
        k: push(
            bucket.at[peer[k], tail], got.at[k - 1, tail], ts.at[k - 1], tr.at[k - 1], (peer[k], gy)
        )
        for k in ORDER
    }
    for n, (k, (first, second)) in enumerate(VIA.items()):
        hops[k] = push(bucket.at[peer[k], head], relay.at[n], hs.at[n], hr.at[n], (peer[first], gy))
        sent[k] = push(relay.at[n], got.at[k - 1, head], xs.at[k - 1], xr.at[k - 1], (peer[second], gy))

    onward = []

    def forward(k, src, src_meta):
        made = [
            push(src_meta, pair_meta.at[k], zms.at[k], zmr.at[k], partner),
            push(src, pair.at[k], zs.at[k], zr.at[k], partner),
        ]
        for c in made:
            c.start()
        onward.extend(made)

    def keep_tags(k, src):
        c = pltpu.make_async_copy(src, tags.at[k], ms.at[k])
        c.start()
        c.wait()

    sent[ORDER[0]].start()
    forward(0, bucket.at[gx, pl.ds(0, HEAD)], meta.at[gx])
    for k in ORDER[1:]:
        hops.get(k, sent[k]).start()
    keep_tags(0, meta.at[gx])
    for k in ORDER:
        sent_meta[k].wait_recv()
        keep_tags(k, got_meta.at[k - 1])
    counts = [tags[k, 0, COUNT] for k in range(n_gx)]
    beyond = [jnp.maximum(n - HEAD, 0) for n in counts]
    starts = [0]
    for n in beyond:
        starts.append(starts[-1] + n)
    bad = jnp.where(starts[-1] > EXTRA, 1, 0)
    for n in counts:
        bad = jnp.maximum(bad, jnp.where(n > LEAN, 1, 0))
    ballots[0] = jnp.zeros((8, 128), jnp.int32) + bad

    votes = []

    def vote(n):
        c = push(ballots.at[n], heard.at[n], vs.at[n], vr.at[n], voters[n])
        c.start()
        votes.append(c)

    def count(n):
        votes[n].wait_recv()
        ballots[n + 1] = jnp.maximum(ballots[n], heard[n])

    for n, k in enumerate(ORDER):
        if k == AFTER:
            for j in VIA:
                hops[j].wait_recv()
                sent[j].start()
            for j in ORDER:
                ends[j].start()
        sent[k].wait_recv()
        forward(k, got.at[k - 1, pl.ds(0, HEAD)], got_meta.at[k - 1])
        if n == 3:
            count(0)
        if n == 5:
            count(1)
        if n in (1, 3):
            vote(n // 2)
    for k in ORDER:
        ends[k].wait_recv()
    for p in range(EXTRA):
        k, n = 0, p
        for j in range(1, n_gx):
            past = p >= starts[j]
            k = jnp.where(past, j, k)
            n = jnp.where(past, p - starts[j], n)
        at = HEAD + jnp.minimum(n, TAIL - 1)
        spare[p] = jnp.where(k == 0, bucket[gx, at], got[jnp.maximum(k, 1) - 1, at])
    rest = push(spare, extra, es, er, partner)
    rest.start()
    for n in range(2, VOTES):
        vote(n)
        count(n)
    out = pltpu.make_async_copy(ballots.at[VOTES], result, ms.at[0])
    out.start()
    for k in ORDER:
        sent_meta[k].wait_send()
        sent[k].wait_send()
        ends[k].wait_send()
    for k in VIA:
        hops[k].wait_send()
    for c in votes:
        c.wait_send()
    out.wait()
    over[0, 0] = result[0, 0]
    for c in onward:
        c.wait()
    rest.wait()


def lean_route(n_gx, bucket, meta):
    data = lambda n, cap: jax.ShapeDtypeStruct((n, cap, 32, 128), F32)
    tags = lambda n: jax.ShapeDtypeStruct((n, 1, META), jnp.int32)
    sems = lambda *n: pltpu.SemaphoreType.DMA(n)
    return pl.pallas_call(
        lean_kernel,
        out_shape=(
            data(n_gx - 1, LEAN),
            tags(n_gx - 1),
            data(n_gx, HEAD),
            tags(n_gx),
            jax.ShapeDtypeStruct((EXTRA, 32, 128), F32),
            jax.ShapeDtypeStruct((1, 1), jnp.int32),
        ),
        in_specs=[VMEM, ANY],
        out_specs=[VMEM] + [ANY] * 4 + [SMEM],
        scratch_shapes=[
            pltpu.SMEM((n_gx, 1, META), jnp.int32),
            pltpu.VMEM((EXTRA, 32, 128), F32),
            pltpu.VMEM((len(VIA), HEAD, 32, 128), F32),
            pltpu.VMEM((VOTES + 1, 8, 128), jnp.int32),
            pltpu.VMEM((VOTES, 8, 128), jnp.int32),
            pltpu.SMEM((8, 128), jnp.int32),
        ]
        + [sems(len(VIA))] * 2
        + [sems(n_gx - 1)] * 2
        + [sems(n_gx - 1)] * 4
        + [sems(n_gx)] * 4
        + [sems(), sems(), sems(VOTES), sems(VOTES), sems(n_gx)],
        compiler_params=pltpu.CompilerParams(collective_id=2, has_side_effects=True, vmem_limit_bytes=4 << 20),
        name="lean_route",
    )(bucket, meta)


STEP = 5
PANEL = SLOTS * 16 * 256


def unpack_kernel(n_gx, lean, tags, got_tags, pair_tags, bucket, got, pair, extra, out, *rest):
    panel, osems = rest
    gx, odd = lax.axis_index("gx"), lax.rem(lax.axis_index("gy"), 2)
    own_cap, pair_cap = got.shape[1], pair.shape[1]
    chunks = [(tags, gx, bucket, gx)]
    chunks += [(got_tags, k, got, k) for k in range(n_gx - 1)]
    chunks += [(pair_tags, k, pair, k) for k in range(n_gx)]

    def place(base, tag, block):
        panel[pl.ds(base + tag, 32, 8), :] = block

    stores = []
    for half in range(2):
        base = (odd if half == 0 else 1 - odd) * 2048
        cap = own_cap if half == 0 else pair_cap

        @pl.loop(0, 8)
        def _(g):
            for s in range(SLOTS):
                panel[pl.ds(s * 4096 + base + g * 256, 256), :] = jnp.zeros((256, 128), F32)

        for c in range(n_gx):
            table, k, stage, part = chunks[half * n_gx + c]
            count = jnp.minimum(table[k, 0, COUNT], cap)

            @pl.loop(0, (count + STEP - 1) // STEP)
            def _(b):
                at = [b * STEP + u for u in range(STEP)]
                if not lean:
                    at = [jnp.minimum(n, cap - 1) for n in at]
                found = [stage[part, n] for n in at]
                for u in range(STEP):
                    place(base, table[k, 0, b * STEP + u], found[u])

        if half == 1 and lean:
            at = 0
            for k in range(n_gx):
                beyond = jnp.maximum(pair_tags[k, 0, COUNT] - pair_cap, 0)
                begin = at

                @pl.loop(0, beyond)
                def _(n):
                    place(base, pair_tags[k, 0, pair_cap + n], extra[begin + n])

                at = at + beyond

        for s in range(SLOTS):
            store = pltpu.make_async_copy(
                panel.at[pl.ds(s * 4096 + base, 2048)],
                out.at[pl.ds(s * 4096 + base, 2048)],
                osems.at[half, s],
            )
            store.start()
            stores.append(store)
    for store in stores:
        store.wait()


def unpack(n_gx, lean, tags, got_tags, pair_tags, bucket, got, pair, extra):
    return pl.pallas_call(
        functools.partial(unpack_kernel, n_gx, lean),
        out_shape=jax.ShapeDtypeStruct((PANEL, 128), F32),
        in_specs=[SMEM] * 3 + [VMEM] * 4,
        out_specs=ANY,
        scratch_shapes=[
            pltpu.VMEM((PANEL + 2048 + 256, 128), F32),
            pltpu.SemaphoreType.DMA((2, SLOTS)),
        ],
        compiler_params=pltpu.CompilerParams(vmem_limit_bytes=40 << 20),
        name="unpack_lean" if lean else "unpack_full",
    )(tags, got_tags, pair_tags, bucket, got, pair, extra)


def body(blocks, prolong, columns, aggregate, column_slot, owner_row):
    n_gx, n_gy = lax.axis_size("gx"), lax.axis_size("gy")
    flat = blocks.reshape(NB, NNZ, 32, 128).transpose(0, 2, 1, 3).reshape(NB, 128, 128)
    q = prolong.reshape(16, 8, 32, 128).transpose(0, 2, 1, 3).reshape(16, 256, 128)
    ints = (columns.T, column_slot.T, aggregate.reshape(1, NB))
    nblocks, *near, weights, rows = halo(n_gx, n_gy, flat, q.reshape(16, 32, 8, 128), *ints)
    bucket, meta = coarse_buckets(n_gx, n_gy, owner_row, flat, nblocks, weights, rows, ints, near)
    got, got_meta, pair, pair_meta, extra, over = lean_route(n_gx, bucket, meta)

    def full(_):
        got, got_meta, pair, pair_meta = route(n_gx, bucket, meta)
        return unpack(n_gx, False, meta, got_meta, pair_meta, bucket, got, pair, extra)

    def fitted(_):
        return unpack(n_gx, True, meta, got_meta, pair_meta, bucket, got, pair, extra)

    out = lax.cond(over[0, 0] > 0, full, fitted, 0)
    out = out.reshape(SLOTS, 16, 32, 8, 128).transpose(1, 3, 0, 2, 4)
    return out.reshape(NB, SLOTS, BS * BS)


def solution(mesh):
    placed = (
        P(("gx", "gy"), None, None),
        P(("gx", "gy"), None),
        P(("gx", "gy"), None),
        P(("gx", "gy")),
        P(("gx", "gy"), None),
        P(("gx", "gy")),
    )
    return jax.shard_map(
        body, mesh=mesh, in_specs=placed, out_specs=P(("gx", "gy"), None, None), check_vma=False
    )
```
